256 devices in a mesh: sect: 2 (over core), sec: 128 (over z, y, x).
Axes of the slice: x: 4, y: 4, z: 8, core: 2. Of those that a mesh axis runs over, the one named last changes fastest.
Arguments:
- start_vectors: bfloat16 [2, 2, 128, 4, 256, 256], P('sect', None, 'sec'), may hold values from -20 to 20
- left_env: bfloat16 [2, 128, 5, 256, 256], P('sect', 'sec'), may hold values from -0.15625 to 0.15625
- right_env: bfloat16 [2, 128, 5, 256, 256], P('sect', 'sec'), may hold values from -0.375 to 0.375
- pair_mpo: float32 [5, 5, 4, 4], replicated, may hold values from -1.25 to 1.25
Outputs:
- ritz_vector: float32 [2, 2, 128, 4, 256, 256], P('sect', None, 'sec')
- ritz_residual: float32 [2, 2, 128, 4, 256, 256], P('sect', None, 'sec')
- energy: float32 [2, 2], P('sect')
The draws below stay inside these ranges and needn't reach their ends.
All inputs are finite; a program needn't handle non-finite values.
Results may differ from the reference program's by a relative error of at most 0.0095.
Values may be sent and summed in bfloat16 or wider, within the bound.
A program may use at most 128 MiB of HBM per device.

```python
import jax
import jax.numpy as jnp
from jax import lax

BLOCK = 256
MPO_W = 5
STARTS = 2
SECTORS = 128
SECTIONS = 2


def draw_start_vectors(key, part):
    shape = (SECTIONS, STARTS, SECTORS, 4, BLOCK, BLOCK)
    position = jnp.arange(SECTORS, dtype=jnp.float32) / max(SECTORS - 1, 1)
    values = jax.random.truncated_normal(key, -6.0, 6.0, shape, jnp.float32)
    factor = jnp.power(10.0, 0.5 * position)
    scaled = values * factor[None, None, :, None, None, None]
    return scaled.astype(jnp.bfloat16)


def levels(key, shape, cuts, smallest, largest):
    factor_of = 1.0
    for dim, parts in cuts:
        heights = jax.random.uniform(jax.random.fold_in(jax.random.fold_in(key, 6), dim), (parts,), jnp.float32, smallest / len(cuts), largest / len(cuts))
        factor_of = factor_of * jnp.repeat(jnp.exp(heights), shape[dim] // parts).reshape((-1,) + (1,) * (len(shape) - 1 - dim))
    return factor_of


def scatter_about(key, dims, scale, reach, split=(), held_as=jnp.bfloat16):
    entries = scale * jax.random.normal(key, dims, jnp.float32)
    if split:
        entries = entries * levels(key, dims, split, -0.22, 0.18)
    return jnp.clip(entries, -reach, reach).astype(held_as)


def setup_inputs(seed: int = 0) -> dict:
    key_of = jax.random.split(jax.random.key(seed), 5)
    start_vectors = draw_start_vectors(jax.random.fold_in(key_of[4], 71), 0)
    left_env = scatter_about(key_of[1], (SECTIONS, SECTORS, MPO_W, BLOCK, BLOCK), (MPO_W * BLOCK) ** -0.5, 0.15625, ((0, 2), (1, 128)))
    right_env = scatter_about(key_of[2], (SECTIONS, SECTORS, MPO_W, BLOCK, BLOCK), BLOCK ** -0.5, 0.375, ((0, 2), (1, 128)))
    pair_mpo = scatter_about(key_of[3], (MPO_W, MPO_W, 4, 4), (MPO_W * 4) ** -0.5, 1.25, (), jnp.float32)
    return {"start_vectors": start_vectors, "left_env": left_env, "right_env": right_env, "pair_mpo": pair_mpo}


epsilon = 1e-06
pair_offsets = (0, 1, 1, 2)

def pair_charges():
    return jnp.array([0, 1, 1, 2], jnp.int32)

def channel_shifts(channels):
    series = jnp.arange(channels, dtype=jnp.int32)
    return jnp.where(series == channels - 2, 1, jnp.where(series == channels - 1, -1, 0)).astype(jnp.int32)

def masked_mpo(pair_mpo):
    channels = pair_mpo.shape[0]
    shifts = channel_shifts(channels)
    charges = pair_charges()
    change = charges[:, None] - charges[None, :]
    displaced = shifts[:, None] - shifts[None, :]
    allowed = change[None, None, :, :] == displaced[:, :, None, None]
    return jnp.where(allowed, pair_mpo, jnp.float32(0.0))

def sector_masks(sector_ids, sector_total, channels):
    shifts = channel_shifts(channels)
    charges = pair_charges()
    left_target = sector_ids[:, None] + shifts[None, :]
    right_source = sector_ids[:, None] - shifts[None, :]
    right_bond = sector_ids[:, None] + charges[None, :] - 1
    left_keep = (left_target >= 0) & (left_target < sector_total)
    right_keep = (right_source >= 0) & (right_source < sector_total)
    block_keep = (right_bond >= 0) & (right_bond < sector_total)
    return (left_keep, right_keep, block_keep)

def effective_apply(vector_b, left_used, right_used, mpo_kept):
    sector_total = left_used.shape[0]
    channels = left_used.shape[1]
    right_padded = jnp.pad(right_used, ((1, 1), (0, 0), (0, 0), (0, 0)))
    partials = []
    for spin_pair in range(4):
        offset = pair_offsets[spin_pair]
        chosen = right_padded[offset:offset + sector_total]
        partials.append(jnp.einsum('vqab,qwcb->vqwac', vector_b[:, :, spin_pair].astype(jnp.float32), chosen.astype(jnp.float32)))
    stacked = jnp.stack(partials, axis=2)
    blended = jnp.einsum('wxts,vqsxac->vqtwac', mpo_kept, stacked, precision=lax.Precision.HIGHEST).astype(jnp.bfloat16)
    padded = jnp.pad(blended, ((0, 0), (1, 1), (0, 0), (0, 0), (0, 0), (0, 0)))
    columns = []
    for channel in range(channels):
        displaced = 1 if channel == channels - 2 else -1 if channel == channels - 1 else 0
        columns.append(padded[:, 1 + displaced:1 + displaced + sector_total, :, channel])
    selected = jnp.stack(columns, axis=3)
    return jnp.einsum('qwab,vqswbc->vqsac', left_used.astype(jnp.float32), selected.astype(jnp.float32))

def totals(values):
    return lax.optimization_barrier(jnp.sum(values, axis=(1, 2, 3, 4)))

def spread(scalars):
    return scalars[:, None, None, None, None]

def davidson(start, left_used, right_used, mpo_kept):
    sector_total = left_used.shape[0]
    channels = left_used.shape[1]
    sector_ids = jnp.arange(sector_total, dtype=jnp.int32)
    left_keep, right_keep, block_keep = sector_masks(sector_ids, sector_total, channels)
    zero_half = jnp.zeros((), jnp.bfloat16)
    left_used = jnp.where(left_keep[:, :, None, None], left_used, zero_half)
    right_used = jnp.where(right_keep[:, :, None, None], right_used, zero_half)
    start_f = start.astype(jnp.float32) * block_keep[None, :, :, None, None].astype(jnp.float32)
    start_sq = totals(start_f * start_f)
    vector_b = (start_f / spread(jnp.sqrt(start_sq + epsilon))).astype(jnp.bfloat16)
    vector_v = lax.optimization_barrier(vector_b).astype(jnp.float32)
    image_v = effective_apply(vector_b, left_used, right_used, mpo_kept)
    rayleigh = totals(vector_v * image_v)
    residual_v = image_v - spread(rayleigh) * vector_v
    residual_sq = totals(residual_v * residual_v)
    second_b = (residual_v / spread(jnp.sqrt(residual_sq + epsilon))).astype(jnp.bfloat16)
    second_v = lax.optimization_barrier(second_b).astype(jnp.float32)
    image_u = effective_apply(second_b, left_used, right_used, mpo_kept)
    coupling = totals(vector_v * image_u)
    second_diag = totals(second_v * image_u)
    half_gap = 0.5 * (second_diag - rayleigh)
    energy = 0.5 * (rayleigh + second_diag) - jnp.sqrt(half_gap * half_gap + coupling * coupling)
    rotation = 0.5 * jnp.arctan2(coupling, half_gap)
    first_coef = jnp.cos(rotation)
    second_coef = -jnp.sin(rotation)
    ritz_vector = spread(first_coef) * vector_v + spread(second_coef) * second_v
    ritz_residual = spread(first_coef) * image_v + spread(second_coef) * image_u - spread(energy) * ritz_vector
    return (ritz_vector, ritz_residual, energy)

def reference(start_vectors, left_env, right_env, pair_mpo):
    mpo_kept = masked_mpo(pair_mpo)
    left_used = jnp.roll(left_env, 1, axis=0)
    right_used = jnp.roll(right_env, -1, axis=0)

    def section(inputs):
        return davidson(inputs[0], inputs[1], inputs[2], mpo_kept)
    ritz_vector, ritz_residual, energy = lax.map(section, (start_vectors, left_used, right_used))
    return (ritz_vector, ritz_residual, energy)
```

```python
import jax
import jax.numpy as jnp
from jax import lax
from jax.experimental import pallas as pl
from jax.experimental.pallas import tpu as pltpu
from jax.sharding import PartitionSpec as P

MESH = pl.DeviceIdType.MESH
F32 = jnp.float32
BF16 = jnp.bfloat16
EPSILON = 1e-06
CHARGE = (0, 1, 1, 2)
SHIFT = (0, 0, 0, 1, -1)
SLOT_OF = {0: 0, 3: 1, 1: 2, 2: 3}
SPIN_OF = (0, 3, 1, 2)


def couplings(spin, channel, spin_in):
    change = CHARGE[spin] - CHARGE[spin_in]
    return [w2 for w2 in range(5) if change == SHIFT[channel] - SHIFT[w2]]


COEFS = [
    (w2, spin, channel, spin_in)
    for spin in range(4)
    for channel in range(5)
    for spin_in in range(4)
    for w2 in couplings(spin, channel, spin_in)
]
COEF_AT = {key: index for index, key in enumerate(COEFS)}


def grid_sizes(count):
    return {128: (4, 4, 8), 8: (2, 2, 2)}[count]


def folded(value):
    rows, columns = value.shape
    value = value.reshape(rows // 8, 8, columns).sum(axis=0)
    total = value[:, :128]
    for start in range(128, columns, 128):
        total = total + value[:, start : start + 128]
    return total


def whole(value):
    return jnp.sum(jnp.sum(value, axis=1, keepdims=True), axis=0, keepdims=True)


def kernel(
    sizes,
    mpo_ref,
    start_ref,
    left_ref,
    right_ref,
    vector_ref,
    residual_ref,
    energy_ref,
    us,
    xs,
    part,
    right_buf,
    left_buf,
    blended,
    send_buf,
    recv_buf,
    hs,
    out_buf,
    ar_x,
    ar_y,
    ar_z,
    kept,
    coef,
    in_sem,
    r_send,
    r_recv,
    l_send,
    l_recv,
    b_send,
    b_recv,
    ar_send,
    ar_recv,
    out_sem,
):
    size_x, size_y, size_z = sizes
    count = size_x * size_y * size_z
    block = start_ref.shape[-1]
    step_rows = 32
    sect = lax.axis_index("sect")
    sec = lax.axis_index("sec")
    other = 1 - sect
    up = lax.rem(sec + 1, count)
    down = lax.rem(sec + count - 1, count)
    at_x = lax.rem(sec, size_x)
    at_y = lax.rem(sec // size_x, size_y)
    at_z = sec // (size_x * size_y)

    def partner_x(k):
        there = lax.rem(at_x + k, size_x)
        return there, sec - at_x + there

    def partner_y(k):
        there = lax.rem(at_y + k, size_y)
        return there, sec + (there - at_y) * size_x

    def partner_z(k):
        there = lax.rem(at_z + k, size_z)
        return there, sec + (there - at_z) * (size_x * size_y)

    def device(section, sector):
        return {"sect": section, "sec": sector}

    def remote(source, target, send_sem, recv_sem, where):
        return pltpu.make_async_remote_copy(
            src_ref=source,
            dst_ref=target,
            send_sem=send_sem,
            recv_sem=recv_sem,
            device_id=where,
            device_id_type=MESH,
        )

    loads = [
        pltpu.make_async_copy(start_ref.at[0, v, 0], us.at[v], in_sem.at[v]) for v in range(2)
    ]
    for load in loads:
        load.start()

    barrier = pltpu.get_barrier_semaphore()
    greeted = [device(other, sec), device(other, up), device(other, down)]
    greeted += [device(sect, up), device(sect, down)]
    greeted += [device(sect, partner_x(k)[1]) for k in range(1, size_x)]
    greeted += [device(sect, partner_y(k)[1]) for k in range(1, size_y)]
    greeted += [device(sect, partner_z(k)[1]) for k in range(1, size_z)]
    for where in greeted:
        pl.semaphore_signal(barrier, inc=1, device_id=where, device_id_type=MESH)
    pl.semaphore_wait(barrier, len(greeted))

    def right_copy(slot, part):
        first, last = ((3, 5), (0, 3))[part]
        return remote(
            right_ref.at[0, 0, first:last],
            right_buf.at[slot, first:last],
            r_send.at[slot, part],
            r_recv.at[slot, part],
            device(other, (up, sec, down)[slot]),
        )

    def left_copy(channel):
        return remote(
            left_ref.at[0, 0, channel],
            left_buf.at[:, channel * block : (channel + 1) * block],
            l_send.at[channel],
            l_recv.at[channel],
            device(other, sec),
        )

    right_copies = [right_copy(*k) for k in ((0, 0), (2, 0), (1, 0), (1, 1), (0, 1), (2, 1))]
    left_copies = [left_copy(channel) for channel in range(5)]
    for copy in right_copies + left_copies:
        copy.start()

    for (w2, spin, channel, spin_in), index in COEF_AT.items():
        there = sec + (CHARGE[spin_in] - 1)
        origin = there - SHIFT[w2]
        keep = (there >= 0) & (there < count) & (origin >= 0) & (origin < count)
        coef[index] = mpo_ref[channel, w2, spin, spin_in] * jnp.where(keep, 1.0, 0.0).astype(F32)

    def multiply(phase, v, spins, channels):
        low, high = spins
        first, last = channels
        right = right_buf[CHARGE[low], first:last].reshape((last - first) * block, block)
        vectors = xs[phase, low:high].reshape((high - low) * block, block)
        product = lax.dot_general(
            vectors, right, (((1,), (1,)), ((), ())), preferred_element_type=F32
        )
        for spin_in in range(low, high):
            for w2 in range(first, last):
                part[v, spin_in, w2] = product[
                    (spin_in - low) * block : (spin_in - low + 1) * block,
                    (w2 - first) * block : (w2 - first + 1) * block,
                ]

    def multiply_all(phase, v):
        multiply(phase, v, (1, 3), (0, 5))
        multiply(phase, v, (0, 1), (0, 5))
        multiply(phase, v, (3, 4), (0, 5))

    def mix(v, targets, store):
        def step(i, carry):
            rows = pl.ds(pl.multiple_of(i * 16, 16), 16)
            held = {}
            for spin, channel in targets:
                total = None
                for spin_in in range(4):
                    for w2 in couplings(spin, channel, spin_in):
                        key = (spin_in, w2)
                        if key not in held:
                            held[key] = part[v, spin_in, w2, rows, :]
                        term = coef[COEF_AT[(w2, spin, channel, spin_in)]] * held[key]
                        total = term if total is None else total + term
                store(spin, channel, rows, i, total.astype(BF16))
            return carry

        lax.fori_loop(0, block // 16, step, 0)

    def block_copy(phase, side, half):
        return remote(
            send_buf.at[phase, side, 2 * half : 2 * half + 2],
            recv_buf.at[phase, 2 * half : 2 * half + 2, side * block : (side + 1) * block],
            b_send.at[phase, side, half],
            b_recv.at[phase, side, half],
            device(sect, (down, up)[side]),
        )

    def produce(phase, v, half):
        def store(spin, channel, rows, i, value):
            send_buf[phase, channel - 3, SLOT_OF[spin], rows, :] = value

        mix(v, [(spin, w) for spin in ((0, 3), (1, 2))[half] for w in (3, 4)], store)
        for side in range(2):
            block_copy(phase, side, half).start()

    def local(phase, v):
        def store(spin, channel, rows, i, value):
            start = pl.multiple_of(channel * block + i * 16, 16)
            blended[spin, pl.ds(start, 16), :] = value

        for channel in range(3):
            mix(v, [(spin, channel) for spin in range(4)], store)
        for spin in range(4):
            hs[phase, spin] = jnp.dot(
                left_buf[:, : 3 * block], blended[spin], preferred_element_type=F32
            )

    def consume(phase):
        for half in range(2):
            for side in range(2):
                block_copy(phase, side, half).wait_recv()
            for slot in (2 * half, 2 * half + 1):
                spin = SPIN_OF[slot]
                hs[phase, spin] += jnp.dot(
                    left_buf[:, 3 * block :],
                    recv_buf[phase, slot],
                    preferred_element_type=F32,
                )

    def over_rows(function, init):
        total = init
        for spin in range(4):

            def step(i, carry, spin=spin):
                rows = pl.ds(pl.multiple_of(i * step_rows, step_rows), step_rows)
                return function(spin, rows, carry)

            total = lax.fori_loop(0, block // step_rows, step, total)
        return total

    zero = jnp.zeros((8, 128), F32)

    def all_reduce(phase, values):
        for index, value in enumerate(values):
            ar_x[phase, at_x, index] = value
        stages = (
            (ar_x, at_x, size_x, partner_x, 0),
            (ar_y, at_y, size_y, partner_y, size_x - 1),
            (ar_z, at_z, size_z, partner_z, size_x + size_y - 2),
        )
        for number, (held, at, size, partner, base) in enumerate(stages):
            copies = []
            arrivals = []
            for k in range(1, size):
                there, sector = partner(k)
                copies.append(
                    remote(
                        held.at[phase, at],
                        held.at[phase, at],
                        ar_send.at[phase, base + k - 1],
                        ar_recv.at[phase, number, at],
                        device(sect, sector),
                    )
                )
                arrivals.append(
                    remote(
                        held.at[phase, there],
                        held.at[phase, there],
                        ar_send.at[phase, base + k - 1],
                        ar_recv.at[phase, number, there],
                        device(sect, sector),
                    )
                )
            for copy in copies:
                copy.start()
            for arrival in arrivals:
                arrival.wait_recv()
            totals = held[phase, 0]
            for index in range(1, size):
                totals = totals + held[phase, index]
            for copy in copies:
                copy.wait_send()
            if number < 2:
                following, place = stages[number + 1][:2]
                following[phase, place] = totals
        return [whole(totals[index]) for index in range(3)]

    def start_block(v, spin, rows):
        value = us[v, spin, rows, :].astype(F32)
        if spin == 0:
            value = value * jnp.where(sec == 0, 0.0, 1.0).astype(F32)
        if spin == 3:
            value = value * jnp.where(sec == count - 1, 0.0, 1.0).astype(F32)
        return value

    def start_sum(v):
        def step(spin, rows, carry):
            value = start_block(v, spin, rows)
            return carry + folded(value * value)

        return over_rows(step, zero)

    def make_first(v, start_sq):
        inv_norm = 1.0 / jnp.sqrt(start_sq + EPSILON)

        def step(spin, rows, carry):
            xs[v, spin, rows, :] = (start_block(v, spin, rows) * inv_norm).astype(BF16)
            return carry

        over_rows(step, 0)

    def first_sums(v):
        def step(spin, rows, carry):
            squared, product, image_sq = carry
            x = xs[v, spin, rows, :].astype(F32)
            image = hs[v, spin, rows, :]
            return (
                squared + folded(x * x),
                product + folded(x * image),
                image_sq + folded(image * image),
            )

        return over_rows(step, (zero, zero, zero))

    def make_second(v, squared, rayleigh, image_sq):
        estimate = image_sq - 2.0 * rayleigh * rayleigh + rayleigh * rayleigh * squared
        norm = jnp.sqrt(jnp.maximum(estimate, 0.0) + EPSILON)
        inv_norm = 1.0 / norm

        def step(spin, rows, carry):
            x = xs[v, spin, rows, :].astype(F32)
            value = hs[v, spin, rows, :] - rayleigh * x
            xs[v + 2, spin, rows, :] = (value * inv_norm).astype(BF16)
            return carry + folded(value * value)

        kept[v, 0] = jnp.broadcast_to(rayleigh, (8, 128))
        kept[v, 1] = jnp.broadcast_to(norm, (8, 128))
        kept[v, 2] = over_rows(step, zero)

    def second_sums(v):
        def step(spin, rows, carry):
            mixed, diagonal = carry
            x = xs[v, spin, rows, :].astype(F32)
            image = hs[v + 2, spin, rows, :]
            second = xs[v + 2, spin, rows, :].astype(F32)
            return mixed + folded(x * image), diagonal + folded(second * image)

        return over_rows(step, (zero, zero))

    def out_copies(v, spin):
        return [
            pltpu.make_async_copy(
                out_buf.at[which, v, spin], target.at[0, v, 0, spin], out_sem.at[which, v, spin]
            )
            for which, target in enumerate((vector_ref, residual_ref))
        ]

    def finish(v, residual_sq, coupling_raw, diagonal_raw):
        rayleigh = kept[v, 0, 0:1, 0:1]
        scale = kept[v, 1, 0:1, 0:1] / jnp.sqrt(residual_sq + EPSILON)
        coupling = coupling_raw * scale
        second_diag = diagonal_raw * scale * scale
        half_gap = 0.5 * (second_diag - rayleigh)
        radius = jnp.sqrt(half_gap * half_gap + coupling * coupling)
        energy = 0.5 * (rayleigh + second_diag) - radius
        flat = radius <= 0.0
        safe = jnp.where(flat, 1.0, radius)
        larger = jnp.sqrt(0.5 * (1.0 + jnp.abs(half_gap) / safe))
        smaller = 0.5 * jnp.abs(coupling) / (safe * larger)
        ahead = half_gap >= 0.0
        sign = jnp.where(coupling < 0.0, -1.0, 1.0)
        cosine = jnp.where(flat, 1.0, jnp.where(ahead, larger, smaller))
        sine = jnp.where(flat, 0.0, sign * jnp.where(ahead, smaller, larger))
        from_second = -sine * scale

        for spin in range(4):

            def step(i, carry, spin=spin):
                rows = pl.ds(pl.multiple_of(i * step_rows, step_rows), step_rows)
                x = xs[v, spin, rows, :].astype(F32)
                second = xs[v + 2, spin, rows, :].astype(F32)
                ritz = cosine * x + from_second * second
                out_buf[0, v, spin, rows, :] = ritz
                out_buf[1, v, spin, rows, :] = (
                    cosine * hs[v, spin, rows, :]
                    + from_second * hs[v + 2, spin, rows, :]
                    - energy * ritz
                )
                return carry

            lax.fori_loop(0, block // step_rows, step, 0)
            for copy in out_copies(v, spin):
                copy.start()
        energy_ref[0, v] = energy[0, 0]

    for load in loads:
        load.wait()
    for v, total in enumerate(all_reduce(0, (start_sum(0), start_sum(1), zero))[:2]):
        make_first(v, total)
    right_copy(1, 0).wait_recv()
    right_copy(1, 1).wait_recv()
    multiply(0, 0, (1, 3), (0, 5))
    right_copy(0, 0).wait_recv()
    right_copy(2, 0).wait_recv()
    multiply(0, 0, (0, 1), (3, 5))
    multiply(0, 0, (3, 4), (3, 5))
    produce(0, 0, 0)
    right_copy(0, 1).wait_recv()
    right_copy(2, 1).wait_recv()
    multiply(0, 0, (0, 1), (0, 3))
    multiply(0, 0, (3, 4), (0, 3))
    produce(0, 0, 1)
    multiply_all(1, 1)
    produce(1, 1, 0)
    produce(1, 1, 1)
    for copy in left_copies:
        copy.wait_recv()

    @pl.when(sec == count - 1)
    def _():
        left_buf[:, 3 * block : 4 * block] = jnp.zeros((block, block), BF16)

    @pl.when(sec == 0)
    def _():
        left_buf[:, 4 * block :] = jnp.zeros((block, block), BF16)

    def local_step(v, carry):
        local(v, v)
        return carry

    lax.fori_loop(0, 2, local_step, 0)

    def first_step(v, carry):
        consume(v)
        make_second(v, *all_reduce(v + 1, first_sums(v)))
        multiply_all(v + 2, v)
        produce(v + 2, v, 0)
        produce(v + 2, v, 1)
        local(v + 2, v)
        return carry

    lax.fori_loop(0, 2, first_step, 0)

    def second_step(v, carry):
        consume(v + 2)
        mixed, diagonal = second_sums(v)
        finish(v, *all_reduce(v + 3, (kept[v, 2], mixed, diagonal)))
        return carry

    lax.fori_loop(0, 2, second_step, 0)

    for copy in right_copies + left_copies:
        copy.wait_send()
    for phase in range(4):
        for side in range(2):
            for half in range(2):
                block_copy(phase, side, half).wait_send()
    for v in range(2):
        for spin in range(4):
            for copy in out_copies(v, spin):
                copy.wait()


def body(start_vectors, left_env, right_env, pair_mpo):
    block = start_vectors.shape[-1]
    count = lax.axis_size("sec")
    sizes = grid_sizes(count)
    partners = sum(sizes) - 3
    wide = (1, 2, 1, 4, block, block)
    any_spec = pl.BlockSpec(memory_space=pl.ANY)
    smem_spec = pl.BlockSpec(memory_space=pltpu.SMEM)
    dma = pltpu.SemaphoreType.DMA
    return pl.pallas_call(
        lambda *refs: kernel(sizes, *refs),
        name="davidson",
        out_shape=(
            jax.ShapeDtypeStruct(wide, F32),
            jax.ShapeDtypeStruct(wide, F32),
            jax.ShapeDtypeStruct((1, 2), F32),
        ),
        in_specs=[smem_spec, any_spec, any_spec, any_spec],
        out_specs=(any_spec, any_spec, smem_spec),
        scratch_shapes=[
            pltpu.VMEM((2, 4, block, block), BF16),
            pltpu.VMEM((4, 4, block, block), BF16),
            pltpu.VMEM((2, 4, 5, block, block), F32),
            pltpu.VMEM((3, 5, block, block), BF16),
            pltpu.VMEM((block, 5 * block), BF16),
            pltpu.VMEM((4, 3 * block, block), BF16),
            pltpu.VMEM((4, 2, 4, block, block), BF16),
            pltpu.VMEM((4, 4, 2 * block, block), BF16),
            pltpu.VMEM((4, 4, block, block), F32),
            pltpu.VMEM((2, 2, 4, block, block), F32),
            pltpu.VMEM((5, sizes[0], 3, 8, 128), F32),
            pltpu.VMEM((5, sizes[1], 3, 8, 128), F32),
            pltpu.VMEM((5, sizes[2], 3, 8, 128), F32),
            pltpu.VMEM((2, 3, 8, 128), F32),
            pltpu.SMEM((len(COEFS),), F32),
            dma((2,)),
            dma((3, 2)),
            dma((3, 2)),
            dma((5,)),
            dma((5,)),
            dma((4, 2, 2)),
            dma((4, 2, 2)),
            dma((5, partners)),
            dma((5, 3, max(sizes))),
            dma((2, 2, 4)),
        ],
        compiler_params=pltpu.CompilerParams(
            collective_id=0, has_side_effects=True, vmem_limit_bytes=56 * 1024 * 1024
        ),
    )(pair_mpo, start_vectors, left_env, right_env)


def solution(mesh):
    in_specs = (
        P("sect", None, "sec", None, None, None),
        P("sect", "sec", None, None, None),
        P("sect", "sec", None, None, None),
        P(),
    )
    out_specs = (
        P("sect", None, "sec", None, None, None),
        P("sect", None, "sec", None, None, None),
        P("sect", None),
    )
    return jax.shard_map(body, mesh=mesh, in_specs=in_specs, out_specs=out_specs, check_vma=False)
```

```python
import jax
import jax.numpy as jnp
from jax import lax
from jax.experimental import pallas as pl
from jax.experimental.pallas import tpu as pltpu
from jax.sharding import PartitionSpec as P

MESH = pl.DeviceIdType.MESH
F32 = jnp.float32
BF16 = jnp.bfloat16
EPSILON = 1e-06
CHARGE = (0, 1, 1, 2)
SHIFT = (0, 0, 0, 1, -1)
SLOT_OF = {0: 0, 3: 1, 1: 2, 2: 3}
SPIN_OF = (0, 3, 1, 2)


def couplings(spin, channel, spin_in):
    change = CHARGE[spin] - CHARGE[spin_in]
    return [w2 for w2 in range(5) if change == SHIFT[channel] - SHIFT[w2]]


COEFS = [
    (w2, spin, channel, spin_in)
    for spin in range(4)
    for channel in range(5)
    for spin_in in range(4)
    for w2 in couplings(spin, channel, spin_in)
]
COEF_AT = {key: index for index, key in enumerate(COEFS)}


def grid_sizes(count):
    return {128: (16, 8), 8: (4, 2)}[count]


def folded_rows(value):
    return jnp.sum(value, axis=0, keepdims=True)


def folded(value):
    rows, columns = value.shape
    value = value.reshape(rows // 8, 8, columns).sum(axis=0)
    total = value[:, :128]
    for start in range(128, columns, 128):
        total = total + value[:, start : start + 128]
    return total


def whole(value):
    return jnp.sum(jnp.sum(value, axis=1, keepdims=True), axis=0, keepdims=True)


def kernel(
    sizes,
    mpo_ref,
    start_ref,
    left_ref,
    right_ref,
    vector_ref,
    residual_ref,
    energy_ref,
    us,
    xs,
    part,
    right_buf,
    left_buf,
    blended,
    send_buf,
    recv_buf,
    hs,
    out_buf,
    kept,
    coef,
    in_sem,
    r_send,
    r_recv,
    l_send,
    l_recv,
    b_send,
    b_recv,
    ar_send,
    ar_recv,
    out_sem,
    *sums,
):
    count = 1
    for size in sizes:
        count *= size
    block = start_ref.shape[-1]
    step_rows = 32
    sect = lax.axis_index("sect")
    sec = lax.axis_index("sec")
    other = 1 - sect
    up = lax.rem(sec + 1, count)
    down = lax.rem(sec + count - 1, count)
    stages = []
    stride = 1
    for size in sizes:
        stages.append((size, stride, lax.rem(sec // stride, size)))
        stride *= size

    def partner(stage, k):
        size, stride, digit = stages[stage]
        there = lax.rem(digit + k, size)
        return there, sec + (there - digit) * stride

    def device(section, sector):
        return {"sect": section, "sec": sector}

    def remote(source, target, send_sem, recv_sem, where):
        return pltpu.make_async_remote_copy(
            src_ref=source,
            dst_ref=target,
            send_sem=send_sem,
            recv_sem=recv_sem,
            device_id=where,
            device_id_type=MESH,
        )

    barrier = pltpu.get_barrier_semaphore()
    greeted = [device(other, sec), device(other, up), device(other, down)]
    greeted += [device(sect, up), device(sect, down)]
    for stage, size in enumerate(sizes):
        greeted += [device(sect, partner(stage, k)[1]) for k in range(1, size)]
    for where in greeted:
        pl.semaphore_signal(barrier, inc=1, device_id=where, device_id_type=MESH)
    loads = [
        pltpu.make_async_copy(start_ref.at[0, v, 0], us.at[v], in_sem.at[v]) for v in range(2)
    ]
    for load in loads:
        load.start()


    def right_copy(slot, part):
        first, last = ((3, 5), (0, 3))[part]
        return remote(
            right_ref.at[0, 0, first:last],
            right_buf.at[slot, first:last],
            r_send.at[slot, part],
            r_recv.at[slot, part],
            device(other, (up, sec, down)[slot]),
        )

    def left_copy(channel):
        return remote(
            left_ref.at[0, 0, channel],
            left_buf.at[:, channel * block : (channel + 1) * block],
            l_send.at[channel],
            l_recv.at[channel],
            device(other, sec),
        )

    right_copies = [right_copy(*k) for k in ((0, 0), (2, 0), (1, 0), (1, 1), (0, 1), (2, 1))]
    left_copies = [left_copy(channel) for channel in range(5)]

    def multiply(phase, v, spins, channels):
        low, high = spins
        first, last = channels
        right = right_buf[CHARGE[low], first:last].reshape((last - first) * block, block)
        vectors = xs[phase, low:high].reshape((high - low) * block, block)
        product = lax.dot_general(
            vectors, right, (((1,), (1,)), ((), ())), preferred_element_type=F32
        )
        for spin_in in range(low, high):
            for w2 in range(first, last):
                part[v, spin_in, w2] = product[
                    (spin_in - low) * block : (spin_in - low + 1) * block,
                    (w2 - first) * block : (w2 - first + 1) * block,
                ]

    def multiply_all(phase, v):
        multiply(phase, v, (1, 3), (0, 5))
        multiply(phase, v, (0, 1), (0, 5))
        multiply(phase, v, (3, 4), (0, 5))

    def mix(v, targets, store):
        def step(i, carry):
            rows = pl.ds(pl.multiple_of(i * 16, 16), 16)
            held = {}
            for spin, channel in targets:
                total = None
                for spin_in in range(4):
                    for w2 in couplings(spin, channel, spin_in):
                        key = (spin_in, w2)
                        if key not in held:
                            held[key] = part[v, spin_in, w2, rows, :]
                        term = coef[COEF_AT[(w2, spin, channel, spin_in)]] * held[key]
                        total = term if total is None else total + term
                store(spin, channel, rows, i, total.astype(BF16))
            return carry

        lax.fori_loop(0, block // 16, step, 0)

    def block_copy(phase, side, half):
        return remote(
            send_buf.at[phase, side, 2 * half : 2 * half + 2],
            recv_buf.at[phase, 2 * half : 2 * half + 2, side * block : (side + 1) * block],
            b_send.at[phase, side, half],
            b_recv.at[phase, side, half],
            device(sect, (down, up)[side]),
        )

    def produce(phase, v, half):
        def store(spin, channel, rows, i, value):
            send_buf[phase, channel - 3, SLOT_OF[spin], rows, :] = value

        mix(v, [(spin, w) for spin in ((0, 3), (1, 2))[half] for w in (3, 4)], store)

    def send(phase, half):
        for side in range(2):
            block_copy(phase, side, half).start()

    def sent(phase):
        for half in range(2):
            for side in range(2):
                block_copy(phase, side, half).wait_send()

    def local(phase, v):
        def store(spin, channel, rows, i, value):
            start = pl.multiple_of(channel * block + i * 16, 16)
            blended[spin, pl.ds(start, 16), :] = value

        for channel in range(3):
            mix(v, [(spin, channel) for spin in range(4)], store)
        for spin in range(4):
            hs[phase, spin] = jnp.dot(
                left_buf[:, : 3 * block], blended[spin], preferred_element_type=F32
            )

    def consume(phase):
        for half in range(2):
            for side in range(2):
                block_copy(phase, side, half).wait_recv()
            for slot in (2 * half, 2 * half + 1):
                spin = SPIN_OF[slot]
                hs[phase, spin] += jnp.dot(
                    left_buf[:, 3 * block :],
                    recv_buf[phase, slot],
                    preferred_element_type=F32,
                )

    def over_rows(function, init):
        total = init
        for spin in range(4):

            def step(i, carry, spin=spin):
                rows = pl.ds(pl.multiple_of(i * step_rows, step_rows), step_rows)
                return function(spin, rows, carry)

            total = lax.fori_loop(0, block // step_rows, step, total)
        return total

    zero = jnp.zeros((8, 128), F32)

    def sum_copies(phase):
        def copy_to(stage, k):
            digit = stages[stage][2]
            return remote(
                sums[stage].at[phase, digit],
                sums[stage].at[phase, digit],
                ar_send.at[phase, stage, k],
                ar_recv.at[phase, stage, digit],
                device(sect, partner(stage, k)[1]),
            )

        def copy_from(stage, k):
            there, sector = partner(stage, k)
            return remote(
                sums[stage].at[phase, there],
                sums[stage].at[phase, there],
                ar_send.at[phase, stage, k],
                ar_recv.at[phase, stage, there],
                device(sect, sector),
            )

        return copy_to, copy_from

    def send_sums(phase, stage, total):
        copy_to, _ = sum_copies(phase)
        size, _, digit = stages[stage]
        sums[stage][phase, digit] = total
        for k in range(1, size):
            copy_to(stage, k).start()

    def take_sums(phase, stage):
        _, copy_from = sum_copies(phase)
        size = sizes[stage]
        for k in range(1, size):
            copy_from(stage, k).wait_recv()
        total = sums[stage][phase, 0]
        for index in range(1, size):
            total = total + sums[stage][phase, index]
        return total

    def begin_sum(phase, values):
        rows = [folded_rows(value) for value in values]
        rows.append(jnp.zeros((8 - len(rows), 128), F32))
        send_sums(phase, 0, jnp.concatenate(rows, axis=0))

    def pass_sum(phase):
        for stage in range(1, len(sizes)):
            send_sums(phase, stage, take_sums(phase, stage - 1))

    def end_sum(phase):
        total = jnp.sum(take_sums(phase, len(sizes) - 1), axis=1, keepdims=True)
        return [total[k : k + 1, :] for k in range(3)]

    def start_block(v, spin, rows):
        value = us[v, spin, rows, :].astype(F32)
        if spin == 0:
            value = value * jnp.where(sec == 0, 0.0, 1.0).astype(F32)
        if spin == 3:
            value = value * jnp.where(sec == count - 1, 0.0, 1.0).astype(F32)
        return value

    def start_sum(v):
        def step(spin, rows, carry):
            value = start_block(v, spin, rows)
            return carry + folded(value * value)

        return over_rows(step, zero)

    def make_first(v, start_sq):
        inv_norm = 1.0 / jnp.sqrt(start_sq + EPSILON)

        def step(spin, rows, carry):
            xs[v, spin, rows, :] = (start_block(v, spin, rows) * inv_norm).astype(BF16)
            return carry

        over_rows(step, 0)

    def first_sums(v):
        def step(spin, rows, carry):
            squared, product, image_sq = carry
            x = xs[v, spin, rows, :].astype(F32)
            image = hs[v, spin, rows, :]
            return (
                squared + folded(x * x),
                product + folded(x * image),
                image_sq + folded(image * image),
            )

        return over_rows(step, (zero, zero, zero))

    def make_second(v, squared, rayleigh, image_sq):
        estimate = image_sq - 2.0 * rayleigh * rayleigh + rayleigh * rayleigh * squared
        norm = jnp.sqrt(jnp.maximum(estimate, 0.0) + EPSILON)
        inv_norm = 1.0 / norm

        def step(spin, rows, carry):
            x = xs[v, spin, rows, :].astype(F32)
            value = hs[v, spin, rows, :] - rayleigh * x
            xs[v + 2, spin, rows, :] = (value * inv_norm).astype(BF16)
            return carry + folded(value * value)

        kept[v, 0] = jnp.broadcast_to(rayleigh, (8, 128))
        kept[v, 1] = jnp.broadcast_to(norm, (8, 128))
        kept[v, 2] = over_rows(step, zero)

    def second_sums(v):
        def step(spin, rows, carry):
            mixed, diagonal = carry
            x = xs[v, spin, rows, :].astype(F32)
            image = hs[v + 2, spin, rows, :]
            second = xs[v + 2, spin, rows, :].astype(F32)
            return mixed + folded(x * image), diagonal + folded(second * image)

        return over_rows(step, (zero, zero))

    def out_copies(v, spin):
        return [
            pltpu.make_async_copy(
                out_buf.at[which, v, spin], target.at[0, v, 0, spin], out_sem.at[which, v, spin]
            )
            for which, target in enumerate((vector_ref, residual_ref))
        ]

    def finish(v, residual_sq, coupling_raw, diagonal_raw):
        rayleigh = kept[v, 0, 0:1, 0:1]
        scale = kept[v, 1, 0:1, 0:1] / jnp.sqrt(residual_sq + EPSILON)
        coupling = coupling_raw * scale
        second_diag = diagonal_raw * scale * scale
        half_gap = 0.5 * (second_diag - rayleigh)
        radius = jnp.sqrt(half_gap * half_gap + coupling * coupling)
        energy = 0.5 * (rayleigh + second_diag) - radius
        flat = radius <= 0.0
        safe = jnp.where(flat, 1.0, radius)
        larger = jnp.sqrt(0.5 * (1.0 + jnp.abs(half_gap) / safe))
        smaller = 0.5 * jnp.abs(coupling) / (safe * larger)
        ahead = half_gap >= 0.0
        sign = jnp.where(coupling < 0.0, -1.0, 1.0)
        cosine = jnp.where(flat, 1.0, jnp.where(ahead, larger, smaller))
        sine = jnp.where(flat, 0.0, sign * jnp.where(ahead, smaller, larger))
        from_second = -sine * scale

        for spin in range(4):

            def step(i, carry, spin=spin):
                rows = pl.ds(pl.multiple_of(i * step_rows, step_rows), step_rows)
                x = xs[v, spin, rows, :].astype(F32)
                second = xs[v + 2, spin, rows, :].astype(F32)
                ritz = cosine * x + from_second * second
                out_buf[0, v, spin, rows, :] = ritz
                out_buf[1, v, spin, rows, :] = (
                    cosine * hs[v, spin, rows, :]
                    + from_second * hs[v + 2, spin, rows, :]
                    - energy * ritz
                )
                return carry

            lax.fori_loop(0, block // step_rows, step, 0)
            for copy in out_copies(v, spin):
                copy.start()
        energy_ref[0, v] = energy[0, 0]

    for load in loads:
        load.wait()
    start_sq = [start_sum(v) for v in range(2)]
    pl.semaphore_wait(barrier, len(greeted))
    begin_sum(0, start_sq)
    for copy in right_copies + left_copies:
        copy.start()
    for (w2, spin, channel, spin_in), index in COEF_AT.items():
        there = sec + (CHARGE[spin_in] - 1)
        origin = there - SHIFT[w2]
        keep = (there >= 0) & (there < count) & (origin >= 0) & (origin < count)
        coef[index] = mpo_ref[channel, spin][spin_in, w2] * jnp.where(keep, 1.0, 0.0).astype(F32)

    pass_sum(0)
    right_copy(1, 0).wait_recv()
    right_copy(1, 1).wait_recv()
    start_sq = end_sum(0)
    make_first(0, start_sq[0])

    multiply(0, 0, (1, 3), (0, 5))
    right_copy(0, 0).wait_recv()
    right_copy(2, 0).wait_recv()
    multiply(0, 0, (0, 1), (3, 5))
    multiply(0, 0, (3, 4), (3, 5))
    produce(0, 0, 0)
    right_copy(0, 1).wait_recv()
    right_copy(2, 1).wait_recv()
    send(0, 0)
    multiply(0, 0, (0, 1), (0, 3))
    multiply(0, 0, (3, 4), (0, 3))
    produce(0, 0, 1)
    send(0, 1)
    make_first(1, start_sq[1])
    multiply_all(1, 1)
    produce(1, 1, 0)
    produce(1, 1, 1)
    for copy in left_copies:
        copy.wait_recv()

    @pl.when(sec == count - 1)
    def _():
        left_buf[:, 3 * block : 4 * block] = jnp.zeros((block, block), BF16)

    @pl.when(sec == 0)
    def _():
        left_buf[:, 4 * block :] = jnp.zeros((block, block), BF16)

    local(0, 0)
    sent(0)
    send(1, 0)
    send(1, 1)
    consume(0)
    begin_sum(1, first_sums(0))
    local(1, 1)
    pass_sum(1)
    make_second(0, *end_sum(1))

    multiply_all(2, 0)
    produce(2, 0, 0)
    sent(1)
    send(2, 0)
    produce(2, 0, 1)
    send(2, 1)
    consume(1)
    begin_sum(2, first_sums(1))
    local(2, 0)
    pass_sum(2)
    make_second(1, *end_sum(2))
    multiply_all(3, 1)
    produce(3, 1, 0)
    sent(2)
    send(3, 0)
    produce(3, 1, 1)
    send(3, 1)
    consume(2)
    begin_sum(3, (kept[0, 2], *second_sums(0)))
    local(3, 1)
    pass_sum(3)
    finish(0, *end_sum(3))
    consume(3)
    begin_sum(4, (kept[1, 2], *second_sums(1)))
    pass_sum(4)
    finish(1, *end_sum(4))

    sent(3)
    for copy in right_copies + left_copies:
        copy.wait_send()

    def sums_sent(phase, carry):
        copy_to, _ = sum_copies(phase)
        for stage, size in enumerate(sizes):
            for k in range(1, size):
                copy_to(stage, k).wait_send()
        return carry

    lax.fori_loop(0, 5, sums_sent, 0)
    for v in range(2):
        for spin in range(4):
            for copy in out_copies(v, spin):
                copy.wait()


def body(start_vectors, left_env, right_env, pair_mpo):
    block = start_vectors.shape[-1]
    count = lax.axis_size("sec")
    sizes = grid_sizes(count)
    wide = (1, 2, 1, 4, block, block)
    any_spec = pl.BlockSpec(memory_space=pl.ANY)
    vmem_spec = pl.BlockSpec(memory_space=pltpu.VMEM)
    smem_spec = pl.BlockSpec(memory_space=pltpu.SMEM)
    dma = pltpu.SemaphoreType.DMA
    return pl.pallas_call(
        lambda *refs: kernel(sizes, *refs),
        name="davidson",
        out_shape=(
            jax.ShapeDtypeStruct(wide, F32),
            jax.ShapeDtypeStruct(wide, F32),
            jax.ShapeDtypeStruct((1, 2), F32),
        ),
        in_specs=[vmem_spec, any_spec, any_spec, any_spec],
        out_specs=(any_spec, any_spec, smem_spec),
        scratch_shapes=[
            pltpu.VMEM((2, 4, block, block), BF16),
            pltpu.VMEM((4, 4, block, block), BF16),
            pltpu.VMEM((2, 4, 5, block, block), F32),
            pltpu.VMEM((3, 5, block, block), BF16),
            pltpu.VMEM((block, 5 * block), BF16),
            pltpu.VMEM((4, 3 * block, block), BF16),
            pltpu.VMEM((4, 2, 4, block, block), BF16),
            pltpu.VMEM((4, 4, 2 * block, block), BF16),
            pltpu.VMEM((4, 4, block, block), F32),
            pltpu.VMEM((2, 2, 4, block, block), F32),
            pltpu.VMEM((2, 3, 8, 128), F32),
            pltpu.SMEM((len(COEFS),), F32),
            dma((2,)),
            dma((3, 2)),
            dma((3, 2)),
            dma((5,)),
            dma((5,)),
            dma((4, 2, 2)),
            dma((4, 2, 2)),
            dma((5, len(sizes), max(sizes))),
            dma((5, len(sizes), max(sizes))),
            dma((2, 2, 4)),
            *[pltpu.VMEM((5, size, 8, 128), F32) for size in sizes],
        ],
        compiler_params=pltpu.CompilerParams(
            collective_id=0, has_side_effects=True, vmem_limit_bytes=56 * 1024 * 1024
        ),
    )(jnp.transpose(pair_mpo, (0, 2, 3, 1)), start_vectors, left_env, right_env)


def solution(mesh):
    in_specs = (
        P("sect", None, "sec", None, None, None),
        P("sect", "sec", None, None, None),
        P("sect", "sec", None, None, None),
        P(),
    )
    out_specs = (
        P("sect", None, "sec", None, None, None),
        P("sect", None, "sec", None, None, None),
        P("sect", None),
    )
    return jax.shard_map(body, mesh=mesh, in_specs=in_specs, out_specs=out_specs, check_vma=False)
```

```python
import jax
import jax.numpy as jnp
from jax import lax
from jax.experimental import pallas as pl
from jax.experimental.pallas import tpu as pltpu
from jax.sharding import PartitionSpec as P

MESH = pl.DeviceIdType.MESH
F32 = jnp.float32
BF16 = jnp.bfloat16
EPSILON = 1e-06
CHARGE = (0, 1, 1, 2)
SHIFT = (0, 0, 0, 1, -1)
SLOT_OF = {0: 0, 3: 1, 1: 2, 2: 3}
SPIN_OF = (0, 3, 1, 2)


def couplings(spin, channel, spin_in):
    change = CHARGE[spin] - CHARGE[spin_in]
    return [w2 for w2 in range(5) if change == SHIFT[channel] - SHIFT[w2]]


COEFS = [
    (w2, spin, channel, spin_in)
    for spin in range(4)
    for channel in range(5)
    for spin_in in range(4)
    for w2 in couplings(spin, channel, spin_in)
]
COEF_AT = {key: index for index, key in enumerate(COEFS)}


def grid_sizes(count):
    return {128: (16, 8), 8: (4, 2)}[count]


def folded_rows(value):
    return jnp.sum(value, axis=0, keepdims=True)


def folded(value):
    rows, columns = value.shape
    value = value.reshape(rows // 8, 8, columns).sum(axis=0)
    total = value[:, :128]
    for start in range(128, columns, 128):
        total = total + value[:, start : start + 128]
    return total


def whole(value):
    return jnp.sum(jnp.sum(value, axis=1, keepdims=True), axis=0, keepdims=True)


def kernel(
    sizes,
    mpo_ref,
    start_ref,
    left_ref,
    right_ref,
    vector_ref,
    residual_ref,
    energy_ref,
    us,
    xs,
    part,
    right_buf,
    left_buf,
    blended,
    send_buf,
    recv_buf,
    hs,
    out_buf,
    kept,
    coef,
    in_sem,
    r_send,
    r_recv,
    l_send,
    l_recv,
    b_send,
    b_recv,
    ar_send,
    ar_recv,
    out_sem,
    *sums,
):
    count = 1
    for size in sizes:
        count *= size
    block = start_ref.shape[-1]
    step_rows = 32
    sect = lax.axis_index("sect")
    sec = lax.axis_index("sec")
    other = 1 - sect
    up = lax.rem(sec + 1, count)
    down = lax.rem(sec + count - 1, count)
    stages = []
    stride = 1
    for size in sizes:
        stages.append((size, stride, lax.rem(sec // stride, size)))
        stride *= size

    partners = [
        [
            (lax.rem(digit + k, size), sec + (lax.rem(digit + k, size) - digit) * stride)
            for k in range(size)
        ]
        for size, stride, digit in stages
    ]

    def partner(stage, k):
        return partners[stage][k]

    def far_first(size):
        inner = 4 if size == 16 else size
        return sorted(
            range(1, size),
            key=lambda k: -min(k % inner, inner - k % inner) - min(k // inner, size // inner - k // inner),
        )

    def device(section, sector):
        return {"sect": section, "sec": sector}

    def remote(source, target, send_sem, recv_sem, where):
        return pltpu.make_async_remote_copy(
            src_ref=source,
            dst_ref=target,
            send_sem=send_sem,
            recv_sem=recv_sem,
            device_id=where,
            device_id_type=MESH,
        )

    barrier = pltpu.get_barrier_semaphore()
    greeted = [device(other, sec), device(other, up), device(other, down)]
    greeted += [device(sect, up), device(sect, down)]
    for stage, size in enumerate(sizes):
        greeted += [device(sect, partner(stage, k)[1]) for k in range(1, size)]
    for where in greeted:
        pl.semaphore_signal(barrier, inc=1, device_id=where, device_id_type=MESH)
    loads = [
        pltpu.make_async_copy(start_ref.at[0, v, 0], us.at[v], in_sem.at[v]) for v in range(2)
    ]
    for load in loads:
        load.start()


    def right_copy(slot, part):
        first, last = ((3, 5), (0, 3))[part]
        return remote(
            right_ref.at[0, 0, first:last],
            right_buf.at[slot, first:last],
            r_send.at[slot, part],
            r_recv.at[slot, part],
            device(other, (up, sec, down)[slot]),
        )

    def left_copy(channel):
        return remote(
            left_ref.at[0, 0, channel],
            left_buf.at[:, channel * block : (channel + 1) * block],
            l_send.at[channel],
            l_recv.at[channel],
            device(other, sec),
        )

    right_copies = [right_copy(*k) for k in ((0, 0), (2, 0), (1, 0), (1, 1), (0, 1), (2, 1))]
    left_copies = [left_copy(channel) for channel in range(5)]

    def multiply(phase, v, spins, channels):
        low, high = spins
        first, last = channels
        right = right_buf[CHARGE[low], first:last].reshape((last - first) * block, block)
        vectors = xs[phase, low:high].reshape((high - low) * block, block)
        product = lax.dot_general(
            vectors, right, (((1,), (1,)), ((), ())), preferred_element_type=F32
        )
        for spin_in in range(low, high):
            for w2 in range(first, last):
                part[v, spin_in, w2] = product[
                    (spin_in - low) * block : (spin_in - low + 1) * block,
                    (w2 - first) * block : (w2 - first + 1) * block,
                ]

    def multiply_all(phase, v):
        multiply(phase, v, (1, 3), (0, 5))
        multiply(phase, v, (0, 1), (0, 5))
        multiply(phase, v, (3, 4), (0, 5))

    def mix(v, targets, store):
        def step(i, carry):
            rows = pl.ds(pl.multiple_of(i * 16, 16), 16)
            held = {}
            for spin, channel in targets:
                total = None
                for spin_in in range(4):
                    for w2 in couplings(spin, channel, spin_in):
                        key = (spin_in, w2)
                        if key not in held:
                            held[key] = part[v, spin_in, w2, rows, :]
                        term = coef[COEF_AT[(w2, spin, channel, spin_in)]] * held[key]
                        total = term if total is None else total + term
                store(spin, channel, rows, i, total.astype(BF16))
            return carry

        lax.fori_loop(0, block // 16, step, 0)

    def block_copy(phase, side, piece):
        slot, start = piece // 2, (piece % 2) * (block // 2)
        return remote(
            send_buf.at[phase, side, slot, start : start + block // 2],
            recv_buf.at[phase, slot, side * block + start : side * block + start + block // 2],
            b_send.at[phase, side, piece],
            b_recv.at[phase, side, piece],
            device(sect, (down, up)[side]),
        )

    def produce(phase, v, half):
        def store(spin, channel, rows, i, value):
            send_buf[phase, channel - 3, SLOT_OF[spin], rows, :] = value

        mix(v, [(spin, w) for spin in ((0, 3), (1, 2))[half] for w in (3, 4)], store)

    def send(phase, first, last):
        for piece in range(first, last):
            for side in range(2):
                block_copy(phase, side, piece).start()

    def local(phase, v):
        def store(spin, channel, rows, i, value):
            start = pl.multiple_of(channel * block + i * 16, 16)
            blended[spin, pl.ds(start, 16), :] = value

        for channel in range(3):
            mix(v, [(spin, channel) for spin in range(4)], store)
        for spin in range(4):
            hs[phase, spin] = jnp.dot(
                left_buf[:, : 3 * block], blended[spin], preferred_element_type=F32
            )

    def consume(phase):
        for slot in range(4):
            for piece in (2 * slot, 2 * slot + 1):
                for side in range(2):
                    block_copy(phase, side, piece).wait_recv()
            spin = SPIN_OF[slot]
            hs[phase, spin] += jnp.dot(
                left_buf[:, 3 * block :],
                recv_buf[phase, slot],
                preferred_element_type=F32,
            )

    def over_rows(function, init):
        total = init
        for spin in range(4):

            def step(i, carry, spin=spin):
                rows = pl.ds(pl.multiple_of(i * step_rows, step_rows), step_rows)
                return function(spin, rows, carry)

            total = lax.fori_loop(0, block // step_rows, step, total)
        return total

    zero = jnp.zeros((8, 128), F32)

    def sum_copies(phase):
        def copy_to(stage, k):
            digit = stages[stage][2]
            return remote(
                sums[stage].at[phase, digit],
                sums[stage].at[phase, digit],
                ar_send.at[phase, stage, k],
                ar_recv.at[phase, stage, digit],
                device(sect, partner(stage, k)[1]),
            )

        def copy_from(stage, k):
            there, sector = partner(stage, k)
            return remote(
                sums[stage].at[phase, there],
                sums[stage].at[phase, there],
                ar_send.at[phase, stage, k],
                ar_recv.at[phase, stage, there],
                device(sect, sector),
            )

        return copy_to, copy_from

    def send_sums(phase, stage, total):
        copy_to, _ = sum_copies(phase)
        size, _, digit = stages[stage]
        sums[stage][phase, digit] = total
        for k in far_first(size):
            copy_to(stage, k).start()

    def take_sums(phase, stage):
        _, copy_from = sum_copies(phase)
        size = sizes[stage]
        for k in range(1, size):
            copy_from(stage, k).wait_recv()
        total = sums[stage][phase, 0]
        for index in range(1, size):
            total = total + sums[stage][phase, index]
        return total

    def begin_sum(phase, values):
        rows = [folded_rows(value) for value in values]
        if len(rows) < 8:
            rows.append(jnp.zeros((8 - len(rows), 128), F32))
        send_sums(phase, 0, jnp.concatenate(rows, axis=0))

    def pass_sum(phase):
        for stage in range(1, len(sizes)):
            send_sums(phase, stage, take_sums(phase, stage - 1))

    def end_sum(phase):
        total = jnp.sum(take_sums(phase, len(sizes) - 1), axis=1, keepdims=True)
        return [total[k : k + 1, :] for k in range(6)]

    def start_block(v, spin, rows):
        value = us[v, spin, rows, :].astype(F32)
        if spin == 0:
            value = value * jnp.where(sec == 0, 0.0, 1.0).astype(F32)
        if spin == 3:
            value = value * jnp.where(sec == count - 1, 0.0, 1.0).astype(F32)
        return value

    def start_sum(v):
        def step(spin, rows, carry):
            value = start_block(v, spin, rows)
            return carry + folded(value * value)

        return over_rows(step, zero)

    def make_first(v, start_sq):
        inv_norm = 1.0 / jnp.sqrt(start_sq + EPSILON)

        def step(spin, rows, carry):
            xs[v, spin, rows, :] = (start_block(v, spin, rows) * inv_norm).astype(BF16)
            return carry

        over_rows(step, 0)

    def first_sums(v):
        def step(spin, rows, carry):
            squared, product, image_sq = carry
            x = xs[v, spin, rows, :].astype(F32)
            image = hs[v, spin, rows, :]
            return (
                squared + folded(x * x),
                product + folded(x * image),
                image_sq + folded(image * image),
            )

        return over_rows(step, (zero, zero, zero))

    def make_second(v, squared, rayleigh, image_sq):
        estimate = image_sq - 2.0 * rayleigh * rayleigh + rayleigh * rayleigh * squared
        norm = jnp.sqrt(jnp.maximum(estimate, 0.0) + EPSILON)
        inv_norm = 1.0 / norm

        def step(spin, rows, carry):
            x = xs[v, spin, rows, :].astype(F32)
            value = hs[v, spin, rows, :] - rayleigh * x
            xs[v + 2, spin, rows, :] = (value * inv_norm).astype(BF16)
            return carry + folded(value * value)

        kept[v, 0] = jnp.broadcast_to(rayleigh, (8, 128))
        kept[v, 1] = jnp.broadcast_to(norm, (8, 128))
        kept[v, 2] = over_rows(step, zero)

    def second_sums(v):
        def step(spin, rows, carry):
            mixed, diagonal = carry
            x = xs[v, spin, rows, :].astype(F32)
            image = hs[v + 2, spin, rows, :]
            second = xs[v + 2, spin, rows, :].astype(F32)
            return mixed + folded(x * image), diagonal + folded(second * image)

        return over_rows(step, (zero, zero))

    def out_copies(v, spin):
        return [
            pltpu.make_async_copy(
                out_buf.at[which, v, spin], target.at[0, v, 0, spin], out_sem.at[which, v, spin]
            )
            for which, target in enumerate((vector_ref, residual_ref))
        ]

    def finish(v, residual_sq, coupling_raw, diagonal_raw):
        rayleigh = kept[v, 0, 0:1, 0:1]
        scale = kept[v, 1, 0:1, 0:1] / jnp.sqrt(residual_sq + EPSILON)
        coupling = coupling_raw * scale
        second_diag = diagonal_raw * scale * scale
        half_gap = 0.5 * (second_diag - rayleigh)
        radius = jnp.sqrt(half_gap * half_gap + coupling * coupling)
        energy = 0.5 * (rayleigh + second_diag) - radius
        flat = radius <= 0.0
        safe = jnp.where(flat, 1.0, radius)
        larger = jnp.sqrt(0.5 * (1.0 + jnp.abs(half_gap) / safe))
        smaller = 0.5 * jnp.abs(coupling) / (safe * larger)
        ahead = half_gap >= 0.0
        sign = jnp.where(coupling < 0.0, -1.0, 1.0)
        cosine = jnp.where(flat, 1.0, jnp.where(ahead, larger, smaller))
        sine = jnp.where(flat, 0.0, sign * jnp.where(ahead, smaller, larger))
        from_second = -sine * scale

        for spin in range(4):

            def step(i, carry, spin=spin):
                rows = pl.ds(pl.multiple_of(i * step_rows, step_rows), step_rows)
                x = xs[v, spin, rows, :].astype(F32)
                second = xs[v + 2, spin, rows, :].astype(F32)
                ritz = cosine * x + from_second * second
                out_buf[0, v, spin, rows, :] = ritz
                out_buf[1, v, spin, rows, :] = (
                    cosine * hs[v, spin, rows, :]
                    + from_second * hs[v + 2, spin, rows, :]
                    - energy * ritz
                )
                return carry

            lax.fori_loop(0, block // step_rows, step, 0)
            for copy in out_copies(v, spin):
                copy.start()
        energy_ref[0, v] = energy[0, 0]

    for load in loads:
        load.wait()
    start_sq = [start_sum(v) for v in range(2)]
    pl.semaphore_wait(barrier, len(greeted))
    begin_sum(0, start_sq)
    for copy in right_copies[:4] + left_copies:
        copy.start()
    for (w2, spin, channel, spin_in), index in COEF_AT.items():
        there = sec + (CHARGE[spin_in] - 1)
        origin = there - SHIFT[w2]
        keep = (there >= 0) & (there < count) & (origin >= 0) & (origin < count)
        coef[index] = mpo_ref[channel, spin][spin_in, w2] * jnp.where(keep, 1.0, 0.0).astype(F32)

    pass_sum(0)
    for copy in right_copies[4:]:
        copy.start()
    right_copy(1, 0).wait_recv()
    right_copy(1, 1).wait_recv()
    start_sq = end_sum(0)
    make_first(0, start_sq[0])

    multiply(0, 0, (1, 3), (0, 5))
    right_copy(0, 0).wait_recv()
    right_copy(2, 0).wait_recv()
    multiply(0, 0, (0, 1), (3, 5))
    multiply(0, 0, (3, 4), (3, 5))
    produce(0, 0, 0)
    send(0, 0, 4)
    make_first(1, start_sq[1])
    right_copy(0, 1).wait_recv()
    right_copy(2, 1).wait_recv()
    multiply(0, 0, (0, 1), (0, 3))
    multiply(0, 0, (3, 4), (0, 3))
    produce(0, 0, 1)
    send(0, 4, 8)
    multiply_all(1, 1)
    produce(1, 1, 0)
    send(1, 0, 2)
    produce(1, 1, 1)
    for copy in left_copies:
        copy.wait_recv()

    @pl.when(sec == count - 1)
    def _():
        left_buf[:, 3 * block : 4 * block] = jnp.zeros((block, block), BF16)

    @pl.when(sec == 0)
    def _():
        left_buf[:, 4 * block :] = jnp.zeros((block, block), BF16)

    local(0, 0)
    consume(0)
    begin_sum(1, first_sums(0))
    send(1, 2, 5)
    local(1, 1)
    pass_sum(1)
    send(1, 5, 8)
    make_second(0, *end_sum(1)[:3])

    multiply_all(2, 0)
    produce(2, 0, 0)
    send(2, 0, 2)
    consume(1)
    begin_sum(2, first_sums(1))
    send(2, 2, 4)
    produce(2, 0, 1)
    send(2, 4, 5)
    local(2, 0)
    pass_sum(2)
    send(2, 5, 8)
    make_second(1, *end_sum(2)[:3])
    multiply_all(3, 1)
    produce(3, 1, 0)
    send(3, 0, 4)
    produce(3, 1, 1)
    send(3, 4, 8)
    local(3, 1)
    consume(2)
    first = (kept[0, 2], *second_sums(0))
    consume(3)
    begin_sum(3, (*first, kept[1, 2], *second_sums(1)))
    pass_sum(3)
    final = end_sum(3)
    finish(0, *final[:3])
    finish(1, *final[3:])

    def blocks_sent(phase, carry):
        for piece in range(8):
            for side in range(2):
                block_copy(phase, side, piece).wait_send()
        return carry

    lax.fori_loop(0, 4, blocks_sent, 0)
    for copy in right_copies + left_copies:
        copy.wait_send()

    def sums_sent(phase, carry):
        copy_to, _ = sum_copies(phase)
        for stage, size in enumerate(sizes):
            for k in range(1, size):
                copy_to(stage, k).wait_send()
        return carry

    lax.fori_loop(0, 4, sums_sent, 0)
    for v in range(2):
        for spin in range(4):
            for copy in out_copies(v, spin):
                copy.wait()


def body(start_vectors, left_env, right_env, pair_mpo):
    block = start_vectors.shape[-1]
    count = lax.axis_size("sec")
    sizes = grid_sizes(count)
    wide = (1, 2, 1, 4, block, block)
    any_spec = pl.BlockSpec(memory_space=pl.ANY)
    vmem_spec = pl.BlockSpec(memory_space=pltpu.VMEM)
    smem_spec = pl.BlockSpec(memory_space=pltpu.SMEM)
    dma = pltpu.SemaphoreType.DMA
    return pl.pallas_call(
        lambda *refs: kernel(sizes, *refs),
        name="davidson",
        out_shape=(
            jax.ShapeDtypeStruct(wide, F32),
            jax.ShapeDtypeStruct(wide, F32),
            jax.ShapeDtypeStruct((1, 2), F32),
        ),
        in_specs=[vmem_spec, any_spec, any_spec, any_spec],
        out_specs=(any_spec, any_spec, smem_spec),
        scratch_shapes=[
            pltpu.VMEM((2, 4, block, block), BF16),
            pltpu.VMEM((4, 4, block, block), BF16),
            pltpu.VMEM((2, 4, 5, block, block), F32),
            pltpu.VMEM((3, 5, block, block), BF16),
            pltpu.VMEM((block, 5 * block), BF16),
            pltpu.VMEM((4, 3 * block, block), BF16),
            pltpu.VMEM((4, 2, 4, block, block), BF16),
            pltpu.VMEM((4, 4, 2 * block, block), BF16),
            pltpu.VMEM((4, 4, block, block), F32),
            pltpu.VMEM((2, 2, 4, block, block), F32),
            pltpu.VMEM((2, 3, 8, 128), F32),
            pltpu.SMEM((len(COEFS),), F32),
            dma((2,)),
            dma((3, 2)),
            dma((3, 2)),
            dma((5,)),
            dma((5,)),
            dma((4, 2, 8)),
            dma((4, 2, 8)),
            dma((4, len(sizes), max(sizes))),
            dma((4, len(sizes), max(sizes))),
            dma((2, 2, 4)),
            *[pltpu.VMEM((4, size, 8, 128), F32) for size in sizes],
        ],
        compiler_params=pltpu.CompilerParams(
            collective_id=0, has_side_effects=True, vmem_limit_bytes=56 * 1024 * 1024
        ),
    )(jnp.transpose(pair_mpo, (0, 2, 3, 1)), start_vectors, left_env, right_env)


def solution(mesh):
    in_specs = (
        P("sect", None, "sec", None, None, None),
        P("sect", "sec", None, None, None),
        P("sect", "sec", None, None, None),
        P(),
    )
    out_specs = (
        P("sect", None, "sec", None, None, None),
        P("sect", None, "sec", None, None, None),
        P("sect", None),
    )
    return jax.shard_map(body, mesh=mesh, in_specs=in_specs, out_specs=out_specs, check_vma=False)
```

```python
import jax
import jax.numpy as jnp
from jax import lax
from jax.experimental import pallas as pl
from jax.experimental.pallas import tpu as pltpu
from jax.sharding import PartitionSpec as P

MESH = pl.DeviceIdType.MESH
F32 = jnp.float32
BF16 = jnp.bfloat16
EPSILON = 1e-06
CHARGE = (0, 1, 1, 2)
SHIFT = (0, 0, 0, 1, -1)
SLOT_OF = {0: 0, 3: 1, 1: 2, 2: 3}
SPIN_OF = (0, 3, 1, 2)


def couplings(spin, channel, spin_in):
    change = CHARGE[spin] - CHARGE[spin_in]
    return [w2 for w2 in range(5) if change == SHIFT[channel] - SHIFT[w2]]


COEFS = [
    (w2, spin, channel, spin_in)
    for spin in range(4)
    for channel in range(5)
    for spin_in in range(4)
    for w2 in couplings(spin, channel, spin_in)
]
COEF_AT = {key: index for index, key in enumerate(COEFS)}


def grid_sizes(count):
    return {128: (16, 8), 8: (4, 2)}[count]


def folded_rows(value):
    return jnp.sum(value, axis=0, keepdims=True)


def folded(value):
    rows, columns = value.shape
    value = value.reshape(rows // 8, 8, columns).sum(axis=0)
    total = value[:, :128]
    for start in range(128, columns, 128):
        total = total + value[:, start : start + 128]
    return total


def whole(value):
    return jnp.sum(jnp.sum(value, axis=1, keepdims=True), axis=0, keepdims=True)


def kernel(
    sizes,
    mpo_ref,
    start_ref,
    left_ref,
    right_ref,
    xs,
    hs,
    scalar_ref,
    us,
    part,
    right_buf,
    left_buf,
    blended,
    send_buf,
    recv_buf,
    kept,
    coef,
    in_sem,
    r_send,
    r_recv,
    l_send,
    l_recv,
    b_send,
    b_recv,
    ar_send,
    ar_recv,
    *sums,
):
    count = 1
    for size in sizes:
        count *= size
    block = start_ref.shape[-1]
    step_rows = 32
    sect = lax.axis_index("sect")
    sec = lax.axis_index("sec")
    other = 1 - sect
    up = lax.rem(sec + 1, count)
    down = lax.rem(sec + count - 1, count)
    stages = []
    stride = 1
    for size in sizes:
        stages.append((size, stride, lax.rem(sec // stride, size)))
        stride *= size

    partners = [
        [
            (lax.rem(digit + k, size), sec + (lax.rem(digit + k, size) - digit) * stride)
            for k in range(size)
        ]
        for size, stride, digit in stages
    ]

    def partner(stage, k):
        return partners[stage][k]

    def far_first(size):
        inner = 4 if size == 16 else size
        return sorted(
            range(1, size),
            key=lambda k: -min(k % inner, inner - k % inner) - min(k // inner, size // inner - k // inner),
        )

    def device(section, sector):
        return {"sect": section, "sec": sector}

    def remote(source, target, send_sem, recv_sem, where):
        return pltpu.make_async_remote_copy(
            src_ref=source,
            dst_ref=target,
            send_sem=send_sem,
            recv_sem=recv_sem,
            device_id=where,
            device_id_type=MESH,
        )

    barrier = pltpu.get_barrier_semaphore()
    greeted = [device(other, sec), device(other, up), device(other, down)]
    greeted += [device(sect, up), device(sect, down)]
    for stage, size in enumerate(sizes):
        greeted += [device(sect, partner(stage, k)[1]) for k in range(1, size)]
    for where in greeted:
        pl.semaphore_signal(barrier, inc=1, device_id=where, device_id_type=MESH)
    loads = [
        pltpu.make_async_copy(start_ref.at[0, v, 0], us.at[v], in_sem.at[v]) for v in range(2)
    ]
    for load in loads:
        load.start()


    def right_copy(slot, part):
        first, last = ((3, 5), (0, 3))[part]
        return remote(
            right_ref.at[0, 0, first:last],
            right_buf.at[slot, first:last],
            r_send.at[slot, part],
            r_recv.at[slot, part],
            device(other, (up, sec, down)[slot]),
        )

    def left_copy(channel):
        return remote(
            left_ref.at[0, 0, channel],
            left_buf.at[:, channel * block : (channel + 1) * block],
            l_send.at[channel],
            l_recv.at[channel],
            device(other, sec),
        )

    right_copies = [right_copy(*k) for k in ((0, 0), (2, 0), (1, 0), (1, 1), (0, 1), (2, 1))]
    left_copies = [left_copy(channel) for channel in range(5)]

    def multiply(phase, v, spins, channels):
        low, high = spins
        first, last = channels
        right = right_buf[CHARGE[low], first:last].reshape((last - first) * block, block)
        vectors = xs[phase, low:high].reshape((high - low) * block, block)
        product = lax.dot_general(
            vectors, right, (((1,), (1,)), ((), ())), preferred_element_type=F32
        )
        for spin_in in range(low, high):
            for w2 in range(first, last):
                part[v, spin_in, w2] = product[
                    (spin_in - low) * block : (spin_in - low + 1) * block,
                    (w2 - first) * block : (w2 - first + 1) * block,
                ]

    def multiply_all(phase, v):
        multiply(phase, v, (1, 3), (0, 5))
        multiply(phase, v, (0, 1), (0, 5))
        multiply(phase, v, (3, 4), (0, 5))

    def mix(v, targets, store):
        def step(i, carry):
            rows = pl.ds(pl.multiple_of(i * 16, 16), 16)
            held = {}
            for spin, channel in targets:
                total = None
                for spin_in in range(4):
                    for w2 in couplings(spin, channel, spin_in):
                        key = (spin_in, w2)
                        if key not in held:
                            held[key] = part[v, spin_in, w2, rows, :]
                        term = coef[COEF_AT[(w2, spin, channel, spin_in)]] * held[key]
                        total = term if total is None else total + term
                store(spin, channel, rows, i, total.astype(BF16))
            return carry

        lax.fori_loop(0, block // 16, step, 0)

    def block_copy(phase, side, piece):
        slot, start = piece // 2, (piece % 2) * (block // 2)
        return remote(
            send_buf.at[phase, side, slot, start : start + block // 2],
            recv_buf.at[phase, slot, side * block + start : side * block + start + block // 2],
            b_send.at[phase, side, piece],
            b_recv.at[phase, side, piece],
            device(sect, (down, up)[side]),
        )

    def produce(phase, v, half):
        def store(spin, channel, rows, i, value):
            send_buf[phase, channel - 3, SLOT_OF[spin], rows, :] = value

        mix(v, [(spin, w) for spin in ((0, 3), (1, 2))[half] for w in (3, 4)], store)

    def send(phase, first, last):
        for piece in range(first, last):
            for side in range(2):
                block_copy(phase, side, piece).start()

    def local(phase, v):
        def store(spin, channel, rows, i, value):
            start = pl.multiple_of(channel * block + i * 16, 16)
            blended[spin, pl.ds(start, 16), :] = value

        for channel in range(3):
            mix(v, [(spin, channel) for spin in range(4)], store)
        for spin in range(4):
            hs[phase, spin] = jnp.dot(
                left_buf[:, : 3 * block], blended[spin], preferred_element_type=F32
            )

    def consume(phase):
        for slot in range(4):
            for piece in (2 * slot, 2 * slot + 1):
                for side in range(2):
                    block_copy(phase, side, piece).wait_recv()
            spin = SPIN_OF[slot]
            hs[phase, spin] += jnp.dot(
                left_buf[:, 3 * block :],
                recv_buf[phase, slot],
                preferred_element_type=F32,
            )

    def over_rows(function, init):
        total = init
        for spin in range(4):

            def step(i, carry, spin=spin):
                rows = pl.ds(pl.multiple_of(i * step_rows, step_rows), step_rows)
                return function(spin, rows, carry)

            total = lax.fori_loop(0, block // step_rows, step, total)
        return total

    zero = jnp.zeros((8, 128), F32)

    def sum_copies(phase):
        def copy_to(stage, k):
            digit = stages[stage][2]
            return remote(
                sums[stage].at[phase, digit],
                sums[stage].at[phase, digit],
                ar_send.at[phase, stage, k],
                ar_recv.at[phase, stage, digit],
                device(sect, partner(stage, k)[1]),
            )

        def copy_from(stage, k):
            there, sector = partner(stage, k)
            return remote(
                sums[stage].at[phase, there],
                sums[stage].at[phase, there],
                ar_send.at[phase, stage, k],
                ar_recv.at[phase, stage, there],
                device(sect, sector),
            )

        return copy_to, copy_from

    def send_sums(phase, stage, total):
        copy_to, _ = sum_copies(phase)
        size, _, digit = stages[stage]
        sums[stage][phase, digit] = total
        for k in far_first(size):
            copy_to(stage, k).start()

    def take_sums(phase, stage):
        _, copy_from = sum_copies(phase)
        size = sizes[stage]
        for k in range(1, size):
            copy_from(stage, k).wait_recv()
        total = sums[stage][phase, 0]
        for index in range(1, size):
            total = total + sums[stage][phase, index]
        return total

    def begin_sum(phase, values):
        rows = [folded_rows(value) for value in values]
        if len(rows) < 8:
            rows.append(jnp.zeros((8 - len(rows), 128), F32))
        send_sums(phase, 0, jnp.concatenate(rows, axis=0))

    def pass_sum(phase):
        for stage in range(1, len(sizes)):
            send_sums(phase, stage, take_sums(phase, stage - 1))

    def end_sum(phase):
        total = jnp.sum(take_sums(phase, len(sizes) - 1), axis=1, keepdims=True)
        return [total[k : k + 1, :] for k in range(6)]

    def start_block(v, spin, rows):
        value = us[v, spin, rows, :].astype(F32)
        if spin == 0:
            value = value * jnp.where(sec == 0, 0.0, 1.0).astype(F32)
        if spin == 3:
            value = value * jnp.where(sec == count - 1, 0.0, 1.0).astype(F32)
        return value

    def start_sum(v):
        def step(spin, rows, carry):
            value = start_block(v, spin, rows)
            return carry + folded(value * value)

        return over_rows(step, zero)

    def make_first(v, start_sq):
        inv_norm = 1.0 / jnp.sqrt(start_sq + EPSILON)

        def step(spin, rows, carry):
            xs[v, spin, rows, :] = (start_block(v, spin, rows) * inv_norm).astype(BF16)
            return carry

        over_rows(step, 0)

    def first_sums(v):
        def step(spin, rows, carry):
            squared, product, image_sq = carry
            x = xs[v, spin, rows, :].astype(F32)
            image = hs[v, spin, rows, :]
            return (
                squared + folded(x * x),
                product + folded(x * image),
                image_sq + folded(image * image),
            )

        return over_rows(step, (zero, zero, zero))

    def make_second(v, squared, rayleigh, image_sq):
        estimate = image_sq - 2.0 * rayleigh * rayleigh + rayleigh * rayleigh * squared
        norm = jnp.sqrt(jnp.maximum(estimate, 0.0) + EPSILON)
        inv_norm = 1.0 / norm

        def step(spin, rows, carry):
            x = xs[v, spin, rows, :].astype(F32)
            value = hs[v, spin, rows, :] - rayleigh * x
            xs[v + 2, spin, rows, :] = (value * inv_norm).astype(BF16)
            return carry + folded(value * value)

        kept[v, 0] = jnp.broadcast_to(rayleigh, (8, 128))
        kept[v, 1] = jnp.broadcast_to(norm, (8, 128))
        kept[v, 2] = over_rows(step, zero)

    def second_sums(v):
        def step(spin, rows, carry):
            mixed, diagonal = carry
            x = xs[v, spin, rows, :].astype(F32)
            image = hs[v + 2, spin, rows, :]
            second = xs[v + 2, spin, rows, :].astype(F32)
            return mixed + folded(x * image), diagonal + folded(second * image)

        return over_rows(step, (zero, zero))

    def finish(v, residual_sq, coupling_raw, diagonal_raw):
        rayleigh = kept[v, 0, 0:1, 0:1]
        scale = kept[v, 1, 0:1, 0:1] / jnp.sqrt(residual_sq + EPSILON)
        coupling = coupling_raw * scale
        second_diag = diagonal_raw * scale * scale
        half_gap = 0.5 * (second_diag - rayleigh)
        radius = jnp.sqrt(half_gap * half_gap + coupling * coupling)
        energy = 0.5 * (rayleigh + second_diag) - radius
        flat = radius <= 0.0
        safe = jnp.where(flat, 1.0, radius)
        larger = jnp.sqrt(0.5 * (1.0 + jnp.abs(half_gap) / safe))
        smaller = 0.5 * jnp.abs(coupling) / (safe * larger)
        ahead = half_gap >= 0.0
        sign = jnp.where(coupling < 0.0, -1.0, 1.0)
        cosine = jnp.where(flat, 1.0, jnp.where(ahead, larger, smaller))
        sine = jnp.where(flat, 0.0, sign * jnp.where(ahead, smaller, larger))
        from_second = -sine * scale

        for row, value in enumerate((cosine, from_second, energy)):
            scalar_ref[v, row : row + 1, :] = jnp.broadcast_to(value, (1, 128))

    for load in loads:
        load.wait()
    start_sq = [start_sum(v) for v in range(2)]
    pl.semaphore_wait(barrier, len(greeted))
    begin_sum(0, start_sq)
    for copy in right_copies[:4] + left_copies:
        copy.start()
    for (w2, spin, channel, spin_in), index in COEF_AT.items():
        there = sec + (CHARGE[spin_in] - 1)
        origin = there - SHIFT[w2]
        keep = (there >= 0) & (there < count) & (origin >= 0) & (origin < count)
        coef[index] = mpo_ref[channel, spin][spin_in, w2] * jnp.where(keep, 1.0, 0.0).astype(F32)

    pass_sum(0)
    for copy in right_copies[4:]:
        copy.start()
    right_copy(1, 0).wait_recv()
    right_copy(1, 1).wait_recv()
    start_sq = end_sum(0)
    make_first(0, start_sq[0])

    multiply(0, 0, (1, 3), (0, 5))
    right_copy(0, 0).wait_recv()
    right_copy(2, 0).wait_recv()
    multiply(0, 0, (0, 1), (3, 5))
    multiply(0, 0, (3, 4), (3, 5))
    produce(0, 0, 0)
    send(0, 0, 4)
    make_first(1, start_sq[1])
    right_copy(0, 1).wait_recv()
    right_copy(2, 1).wait_recv()
    multiply(0, 0, (0, 1), (0, 3))
    multiply(0, 0, (3, 4), (0, 3))
    produce(0, 0, 1)
    send(0, 4, 8)
    multiply_all(1, 1)
    produce(1, 1, 0)
    send(1, 0, 2)
    produce(1, 1, 1)
    for copy in left_copies:
        copy.wait_recv()

    @pl.when(sec == count - 1)
    def _():
        left_buf[:, 3 * block : 4 * block] = jnp.zeros((block, block), BF16)

    @pl.when(sec == 0)
    def _():
        left_buf[:, 4 * block :] = jnp.zeros((block, block), BF16)

    local(0, 0)
    consume(0)
    begin_sum(1, first_sums(0))
    send(1, 2, 5)
    local(1, 1)
    pass_sum(1)
    send(1, 5, 8)
    make_second(0, *end_sum(1)[:3])

    multiply_all(2, 0)
    produce(2, 0, 0)
    send(2, 0, 2)
    consume(1)
    begin_sum(2, first_sums(1))
    send(2, 2, 4)
    produce(2, 0, 1)
    send(2, 4, 5)
    local(2, 0)
    pass_sum(2)
    send(2, 5, 8)
    make_second(1, *end_sum(2)[:3])
    multiply_all(3, 1)
    produce(3, 1, 0)
    send(3, 0, 4)
    produce(3, 1, 1)
    send(3, 4, 8)
    local(3, 1)
    consume(2)
    first = (kept[0, 2], *second_sums(0))
    consume(3)
    begin_sum(3, (*first, kept[1, 2], *second_sums(1)))
    pass_sum(3)
    final = end_sum(3)
    finish(0, *final[:3])
    finish(1, *final[3:])

    def blocks_sent(phase, carry):
        for piece in range(8):
            for side in range(2):
                block_copy(phase, side, piece).wait_send()
        return carry

    lax.fori_loop(0, 4, blocks_sent, 0)
    for copy in right_copies + left_copies:
        copy.wait_send()

    def sums_sent(phase, carry):
        copy_to, _ = sum_copies(phase)
        for stage, size in enumerate(sizes):
            for k in range(1, size):
                copy_to(stage, k).wait_send()
        return carry

    lax.fori_loop(0, 4, sums_sent, 0)


def combine(scalar_ref, xs, hs, vector_ref, residual_ref, energy_ref, out_buf, out_sem):
    block = xs.shape[-1]

    def copies(v, spin):
        return [
            pltpu.make_async_copy(
                out_buf.at[which, v, spin], target.at[0, v, 0, spin], out_sem.at[which, v, spin]
            )
            for which, target in enumerate((vector_ref, residual_ref))
        ]

    for v in range(2):
        cosine, from_second, energy = [scalar_ref[v, k : k + 1, 0:1] for k in range(3)]
        for spin in range(4):

            def step(i, carry, v=v, spin=spin):
                rows = pl.ds(pl.multiple_of(i * 32, 32), 32)
                ritz = cosine * xs[v, spin, rows, :].astype(F32)
                ritz = ritz + from_second * xs[v + 2, spin, rows, :].astype(F32)
                out_buf[0, v, spin, rows, :] = ritz
                out_buf[1, v, spin, rows, :] = (
                    cosine * hs[v, spin, rows, :]
                    + from_second * hs[v + 2, spin, rows, :]
                    - energy * ritz
                )
                return carry

            lax.fori_loop(0, block // 32, step, 0)
            for copy in copies(v, spin):
                copy.start()
        energy_ref[0, v] = energy[0, 0]
    for v in range(2):
        for spin in range(4):
            for copy in copies(v, spin):
                copy.wait()


def body(start_vectors, left_env, right_env, pair_mpo):
    block = start_vectors.shape[-1]
    count = lax.axis_size("sec")
    sizes = grid_sizes(count)
    wide = (1, 2, 1, 4, block, block)
    any_spec = pl.BlockSpec(memory_space=pl.ANY)
    vmem_spec = pl.BlockSpec(memory_space=pltpu.VMEM)
    dma = pltpu.SemaphoreType.DMA
    vectors, images, scalars = pl.pallas_call(
        lambda *refs: kernel(sizes, *refs),
        name="davidson",
        out_shape=(
            pltpu.VMEM((4, 4, block, block), BF16),
            pltpu.VMEM((4, 4, block, block), F32),
            pltpu.VMEM((2, 8, 128), F32),
        ),
        in_specs=[vmem_spec, any_spec, any_spec, any_spec],
        out_specs=(vmem_spec, vmem_spec, vmem_spec),
        scratch_shapes=[
            pltpu.VMEM((2, 4, block, block), BF16),
            pltpu.VMEM((2, 4, 5, block, block), F32),
            pltpu.VMEM((3, 5, block, block), BF16),
            pltpu.VMEM((block, 5 * block), BF16),
            pltpu.VMEM((4, 3 * block, block), BF16),
            pltpu.VMEM((4, 2, 4, block, block), BF16),
            pltpu.VMEM((4, 4, 2 * block, block), BF16),
            pltpu.VMEM((2, 3, 8, 128), F32),
            pltpu.SMEM((len(COEFS),), F32),
            dma((2,)),
            dma((3, 2)),
            dma((3, 2)),
            dma((5,)),
            dma((5,)),
            dma((4, 2, 8)),
            dma((4, 2, 8)),
            dma((4, len(sizes), max(sizes))),
            dma((4, len(sizes), max(sizes))),
            *[pltpu.VMEM((4, size, 8, 128), F32) for size in sizes],
        ],
        compiler_params=pltpu.CompilerParams(
            collective_id=0, has_side_effects=True, vmem_limit_bytes=48 * 1024 * 1024
        ),
    )(jnp.transpose(pair_mpo, (0, 2, 3, 1)), start_vectors, left_env, right_env)

    return pl.pallas_call(
        combine,
        name="combine",
        out_shape=(
            jax.ShapeDtypeStruct(wide, F32),
            jax.ShapeDtypeStruct(wide, F32),
            jax.ShapeDtypeStruct((1, 2), F32),
        ),
        in_specs=[vmem_spec, vmem_spec, vmem_spec],
        out_specs=(any_spec, any_spec, pl.BlockSpec(memory_space=pltpu.SMEM)),
        scratch_shapes=[pltpu.VMEM((2, 2, 4, block, block), F32), dma((2, 2, 4))],
        compiler_params=pltpu.CompilerParams(vmem_limit_bytes=16 * 1024 * 1024),
    )(scalars, vectors, images)


def solution(mesh):
    in_specs = (
        P("sect", None, "sec", None, None, None),
        P("sect", "sec", None, None, None),
        P("sect", "sec", None, None, None),
        P(),
    )
    out_specs = (
        P("sect", None, "sec", None, None, None),
        P("sect", None, "sec", None, None, None),
        P("sect", None),
    )
    return jax.shard_map(body, mesh=mesh, in_specs=in_specs, out_specs=out_specs, check_vma=False)
```

```python
import jax
import jax.numpy as jnp
from jax import lax
from jax.experimental import pallas as pl
from jax.experimental.pallas import tpu as pltpu
from jax.sharding import PartitionSpec as P

MESH = pl.DeviceIdType.MESH
F32 = jnp.float32
BF16 = jnp.bfloat16
EPSILON = 1e-06
CHARGE = (0, 1, 1, 2)
SHIFT = (0, 0, 0, 1, -1)
SLOT_OF = {0: 0, 3: 1, 1: 2, 2: 3}
SPIN_OF = (0, 3, 1, 2)


def couplings(spin, channel, spin_in):
    change = CHARGE[spin] - CHARGE[spin_in]
    return [w2 for w2 in range(5) if change == SHIFT[channel] - SHIFT[w2]]


COEFS = [
    (w2, spin, channel, spin_in)
    for spin in range(4)
    for channel in range(5)
    for spin_in in range(4)
    for w2 in couplings(spin, channel, spin_in)
]
COEF_AT = {key: index for index, key in enumerate(COEFS)}


def grid_sizes(count):
    return {128: (16, 8), 8: (4, 2)}[count]


def folded_rows(value):
    return jnp.sum(value, axis=0, keepdims=True)


def folded(value):
    rows, columns = value.shape
    value = value.reshape(rows // 8, 8, columns).sum(axis=0)
    total = value[:, :128]
    for start in range(128, columns, 128):
        total = total + value[:, start : start + 128]
    return total


def whole(value):
    return jnp.sum(jnp.sum(value, axis=1, keepdims=True), axis=0, keepdims=True)


def kernel(
    sizes,
    mpo_ref,
    start_ref,
    left_ref,
    right_ref,
    xs,
    hs,
    scalar_ref,
    us,
    part,
    right_buf,
    left_buf,
    blended,
    send_buf,
    recv_buf,
    kept,
    coef,
    in_sem,
    r_send,
    r_recv,
    l_send,
    l_recv,
    b_send,
    b_recv,
    ar_send,
    ar_recv,
    *sums,
):
    count = 1
    for size in sizes:
        count *= size
    block = start_ref.shape[-1]
    step_rows = 32
    sect = lax.axis_index("sect")
    sec = lax.axis_index("sec")
    other = 1 - sect
    up = lax.rem(sec + 1, count)
    down = lax.rem(sec + count - 1, count)
    stages = []
    stride = 1
    for size in sizes:
        stages.append((size, stride, lax.rem(sec // stride, size)))
        stride *= size

    partners = [
        [
            (lax.rem(digit + k, size), sec + (lax.rem(digit + k, size) - digit) * stride)
            for k in range(size)
        ]
        for size, stride, digit in stages
    ]

    def partner(stage, k):
        return partners[stage][k]

    def far_first(size):
        inner = 4 if size == 16 else size
        return sorted(
            range(1, size),
            key=lambda k: -min(k % inner, inner - k % inner) - min(k // inner, size // inner - k // inner),
        )

    def device(section, sector):
        return {"sect": section, "sec": sector}

    def remote(source, target, send_sem, recv_sem, where):
        return pltpu.make_async_remote_copy(
            src_ref=source,
            dst_ref=target,
            send_sem=send_sem,
            recv_sem=recv_sem,
            device_id=where,
            device_id_type=MESH,
        )

    barrier = pltpu.get_barrier_semaphore()
    greeted = [device(other, sec), device(other, up), device(other, down)]
    greeted += [device(sect, up), device(sect, down)]
    for stage, size in enumerate(sizes):
        greeted += [device(sect, partner(stage, k)[1]) for k in range(1, size)]
    for where in greeted:
        pl.semaphore_signal(barrier, inc=1, device_id=where, device_id_type=MESH)
    loads = [
        pltpu.make_async_copy(start_ref.at[0, v, 0], us.at[v], in_sem.at[v]) for v in range(2)
    ]
    for load in loads:
        load.start()


    def right_copy(slot, part):
        first, last = ((3, 5), (0, 3))[part]
        return remote(
            right_ref.at[0, 0, first:last],
            right_buf.at[slot, first:last],
            r_send.at[slot, part],
            r_recv.at[slot, part],
            device(other, (up, sec, down)[slot]),
        )

    def left_copy(channel):
        return remote(
            left_ref.at[0, 0, channel],
            left_buf.at[:, channel * block : (channel + 1) * block],
            l_send.at[channel],
            l_recv.at[channel],
            device(other, sec),
        )

    right_copies = [right_copy(*k) for k in ((0, 0), (2, 0), (1, 0), (1, 1), (0, 1), (2, 1))]
    left_copies = [left_copy(channel) for channel in range(5)]

    def multiply(phase, v, spins, channels):
        low, high = spins
        first, last = channels
        right = right_buf[CHARGE[low], first:last].reshape((last - first) * block, block)
        vectors = xs[phase, low:high].reshape((high - low) * block, block)
        product = lax.dot_general(
            vectors, right, (((1,), (1,)), ((), ())), preferred_element_type=F32
        )
        for spin_in in range(low, high):
            for w2 in range(first, last):
                part[v, spin_in, w2] = product[
                    (spin_in - low) * block : (spin_in - low + 1) * block,
                    (w2 - first) * block : (w2 - first + 1) * block,
                ]

    def multiply_all(phase, v):
        multiply(phase, v, (1, 3), (0, 5))
        multiply(phase, v, (0, 1), (0, 5))
        multiply(phase, v, (3, 4), (0, 5))

    def multiply_early(phase, v):
        multiply(phase, v, (0, 1), (3, 5))
        multiply(phase, v, (3, 4), (3, 5))
        multiply(phase, v, (1, 3), (0, 3))

    def multiply_late(phase, v):
        multiply(phase, v, (0, 1), (0, 3))
        multiply(phase, v, (3, 4), (0, 3))
        multiply(phase, v, (1, 3), (3, 5))

    def mix(v, targets, store):
        def step(i, carry):
            rows = pl.ds(pl.multiple_of(i * 16, 16), 16)
            held = {}
            for spin, channel in targets:
                total = None
                for spin_in in range(4):
                    for w2 in couplings(spin, channel, spin_in):
                        key = (spin_in, w2)
                        if key not in held:
                            held[key] = part[v, spin_in, w2, rows, :]
                        term = coef[COEF_AT[(w2, spin, channel, spin_in)]] * held[key]
                        total = term if total is None else total + term
                store(spin, channel, rows, i, total.astype(BF16))
            return carry

        lax.fori_loop(0, block // 16, step, 0)

    def block_copy(phase, side, piece):
        slot, start = piece // 2, (piece % 2) * (block // 2)
        return remote(
            send_buf.at[phase, side, slot, start : start + block // 2],
            recv_buf.at[phase, slot, side * block + start : side * block + start + block // 2],
            b_send.at[phase, side, piece],
            b_recv.at[phase, side, piece],
            device(sect, (down, up)[side]),
        )

    def produce(phase, v, half):
        def store(spin, channel, rows, i, value):
            send_buf[phase, channel - 3, SLOT_OF[spin], rows, :] = value

        mix(v, [(spin, w) for spin in ((0, 3), (1, 2))[half] for w in (3, 4)], store)

    def send(phase, first, last):
        for piece in range(first, last):
            for side in range(2):
                block_copy(phase, side, piece).start()

    def local(phase, v):
        def store(spin, channel, rows, i, value):
            start = pl.multiple_of(channel * block + i * 16, 16)
            blended[spin, pl.ds(start, 16), :] = value

        for channel in range(3):
            mix(v, [(spin, channel) for spin in range(4)], store)
        for spin in range(4):
            hs[phase, spin] = jnp.dot(
                left_buf[:, : 3 * block], blended[spin], preferred_element_type=F32
            )

    def spin_rows(spin, function, total):
        def step(i, carry):
            rows = pl.ds(pl.multiple_of(i * step_rows, step_rows), step_rows)
            return function(spin, rows, carry)

        return lax.fori_loop(0, block // step_rows, step, total)

    def over_rows(function, total):
        for spin in range(4):
            total = spin_rows(spin, function, total)
        return total

    def consume(phase, function, total):
        for slot in range(4):
            for piece in (2 * slot, 2 * slot + 1):
                for side in range(2):
                    block_copy(phase, side, piece).wait_recv()
            spin = SPIN_OF[slot]
            hs[phase, spin] += jnp.dot(
                left_buf[:, 3 * block :],
                recv_buf[phase, slot],
                preferred_element_type=F32,
            )
            total = spin_rows(spin, function, total)
        return total

    zero = jnp.zeros((8, 128), F32)

    def sum_copies(phase):
        def copy_to(stage, k):
            digit = stages[stage][2]
            return remote(
                sums[stage].at[phase, digit],
                sums[stage].at[phase, digit],
                ar_send.at[phase, stage, k],
                ar_recv.at[phase, stage, digit],
                device(sect, partner(stage, k)[1]),
            )

        def copy_from(stage, k):
            there, sector = partner(stage, k)
            return remote(
                sums[stage].at[phase, there],
                sums[stage].at[phase, there],
                ar_send.at[phase, stage, k],
                ar_recv.at[phase, stage, there],
                device(sect, sector),
            )

        return copy_to, copy_from

    def send_sums(phase, stage, total):
        copy_to, _ = sum_copies(phase)
        size, _, digit = stages[stage]
        sums[stage][phase, digit] = total
        for k in far_first(size):
            copy_to(stage, k).start()

    def take_sums(phase, stage):
        _, copy_from = sum_copies(phase)
        size = sizes[stage]
        for k in range(1, size):
            copy_from(stage, k).wait_recv()
        total = sums[stage][phase, 0]
        for index in range(1, size):
            total = total + sums[stage][phase, index]
        return total

    def begin_sum(phase, values):
        rows = [folded_rows(value) for value in values]
        rows.append(jnp.zeros((8 - len(rows), 128), F32))
        tile = jnp.sum(jnp.concatenate(rows, axis=0), axis=1, keepdims=True)
        lane = lax.broadcasted_iota(jnp.int32, (8, 128), 1)
        place = lax.broadcasted_iota(jnp.int32, (8, 128), 0)
        spread = jnp.where(lane == place, jnp.broadcast_to(tile, (8, 128)), 0.0)
        send_sums(phase, 0, jnp.sum(spread, axis=0, keepdims=True))

    def pass_sum(phase):
        for stage in range(1, len(sizes)):
            send_sums(phase, stage, take_sums(phase, stage - 1))

    def end_sum(phase):
        total = take_sums(phase, len(sizes) - 1)
        return [total[:, k : k + 1] for k in range(6)]

    def start_block(v, spin, rows):
        value = us[v, spin, rows, :].astype(F32)
        if spin == 0:
            value = value * jnp.where(sec == 0, 0.0, 1.0).astype(F32)
        if spin == 3:
            value = value * jnp.where(sec == count - 1, 0.0, 1.0).astype(F32)
        return value

    def start_sum(v):
        def step(spin, rows, carry):
            value = start_block(v, spin, rows)
            return carry + folded(value * value)

        return over_rows(step, zero)

    def make_first(v, start_sq):
        inv_norm = 1.0 / jnp.sqrt(start_sq + EPSILON)

        def step(spin, rows, carry):
            xs[v, spin, rows, :] = (start_block(v, spin, rows) * inv_norm).astype(BF16)
            return carry

        over_rows(step, 0)

    def first_sums(v):
        def step(spin, rows, carry):
            squared, product, image_sq = carry
            x = xs[v, spin, rows, :].astype(F32)
            image = hs[v, spin, rows, :]
            return (
                squared + folded(x * x),
                product + folded(x * image),
                image_sq + folded(image * image),
            )

        return consume(v, step, (zero, zero, zero))

    def make_second(v, squared, rayleigh, image_sq):
        estimate = image_sq - 2.0 * rayleigh * rayleigh + rayleigh * rayleigh * squared
        norm = jnp.sqrt(jnp.maximum(estimate, 0.0) + EPSILON)
        inv_norm = 1.0 / norm

        def step(spin, rows, carry):
            x = xs[v, spin, rows, :].astype(F32)
            value = hs[v, spin, rows, :] - rayleigh * x
            xs[v + 2, spin, rows, :] = (value * inv_norm).astype(BF16)
            return carry + folded(value * value)

        kept[v, 0] = jnp.broadcast_to(rayleigh, (8, 128))
        kept[v, 1] = jnp.broadcast_to(norm, (8, 128))
        kept[v, 2] = over_rows(step, zero)

    def second_sums(v):
        def step(spin, rows, carry):
            mixed, diagonal = carry
            x = xs[v, spin, rows, :].astype(F32)
            image = hs[v + 2, spin, rows, :]
            second = xs[v + 2, spin, rows, :].astype(F32)
            return mixed + folded(x * image), diagonal + folded(second * image)

        return consume(v + 2, step, (zero, zero))

    def finish(v, residual_sq, coupling_raw, diagonal_raw):
        rayleigh = kept[v, 0, 0:1, 0:1]
        scale = kept[v, 1, 0:1, 0:1] / jnp.sqrt(residual_sq + EPSILON)
        coupling = coupling_raw * scale
        second_diag = diagonal_raw * scale * scale
        half_gap = 0.5 * (second_diag - rayleigh)
        radius = jnp.sqrt(half_gap * half_gap + coupling * coupling)
        energy = 0.5 * (rayleigh + second_diag) - radius
        flat = radius <= 0.0
        safe = jnp.where(flat, 1.0, radius)
        larger = jnp.sqrt(0.5 * (1.0 + jnp.abs(half_gap) / safe))
        smaller = 0.5 * jnp.abs(coupling) / (safe * larger)
        ahead = half_gap >= 0.0
        sign = jnp.where(coupling < 0.0, -1.0, 1.0)
        cosine = jnp.where(flat, 1.0, jnp.where(ahead, larger, smaller))
        sine = jnp.where(flat, 0.0, sign * jnp.where(ahead, smaller, larger))
        from_second = -sine * scale

        for row, value in enumerate((cosine, from_second, energy)):
            scalar_ref[v, row : row + 1, :] = jnp.broadcast_to(value, (1, 128))

    for load in loads:
        load.wait()
    start_sq = [start_sum(v) for v in range(2)]
    pl.semaphore_wait(barrier, len(greeted))
    begin_sum(0, start_sq)
    for copy in right_copies[:4] + left_copies:
        copy.start()
    for (w2, spin, channel, spin_in), index in COEF_AT.items():
        there = sec + (CHARGE[spin_in] - 1)
        origin = there - SHIFT[w2]
        keep = (there >= 0) & (there < count) & (origin >= 0) & (origin < count)
        coef[index] = mpo_ref[channel, spin][spin_in, w2] * jnp.where(keep, 1.0, 0.0).astype(F32)

    pass_sum(0)
    for copy in right_copies[4:]:
        copy.start()
    right_copy(1, 0).wait_recv()
    right_copy(1, 1).wait_recv()
    start_sq = end_sum(0)
    make_first(0, start_sq[0])

    multiply(0, 0, (1, 3), (0, 5))
    right_copy(0, 0).wait_recv()
    right_copy(2, 0).wait_recv()
    multiply(0, 0, (0, 1), (3, 5))
    multiply(0, 0, (3, 4), (3, 5))
    produce(0, 0, 0)
    send(0, 0, 4)
    make_first(1, start_sq[1])
    right_copy(0, 1).wait_recv()
    right_copy(2, 1).wait_recv()
    multiply(0, 0, (0, 1), (0, 3))
    multiply(0, 0, (3, 4), (0, 3))
    produce(0, 0, 1)
    send(0, 4, 8)
    multiply_all(1, 1)
    produce(1, 1, 0)
    send(1, 0, 2)
    produce(1, 1, 1)
    for copy in left_copies:
        copy.wait_recv()

    @pl.when(sec == count - 1)
    def _():
        left_buf[:, 3 * block : 4 * block] = jnp.zeros((block, block), BF16)

    @pl.when(sec == 0)
    def _():
        left_buf[:, 4 * block :] = jnp.zeros((block, block), BF16)

    local(0, 0)
    begin_sum(1, first_sums(0))
    send(1, 2, 8)
    local(1, 1)
    pass_sum(1)
    first = end_sum(1)
    begin_sum(2, first_sums(1))
    make_second(0, *first[:3])

    multiply_early(2, 0)
    produce(2, 0, 0)
    send(2, 0, 4)
    multiply_late(2, 0)
    produce(2, 0, 1)
    send(2, 4, 6)
    pass_sum(2)
    send(2, 6, 8)
    local(2, 0)
    make_second(1, *end_sum(2)[:3])
    multiply_early(3, 1)
    produce(3, 1, 0)
    send(3, 0, 4)
    multiply_late(3, 1)
    produce(3, 1, 1)
    send(3, 4, 8)
    local(3, 1)
    first = (kept[0, 2], *second_sums(0))
    begin_sum(3, (*first, kept[1, 2], *second_sums(1)))

    def blocks_sent(phase, carry):
        for piece in range(8):
            for side in range(2):
                block_copy(phase, side, piece).wait_send()
        return carry

    lax.fori_loop(0, 4, blocks_sent, 0)
    for copy in right_copies + left_copies:
        copy.wait_send()

    def sums_sent(phase, carry):
        copy_to, _ = sum_copies(phase)
        for stage, size in enumerate(sizes):
            for k in range(1, size):
                copy_to(stage, k).wait_send()
        return carry

    lax.fori_loop(0, 3, sums_sent, 0)

    pass_sum(3)
    final = end_sum(3)
    finish(0, *final[:3])
    finish(1, *final[3:])
    sums_sent(3, 0)


def combine(scalar_ref, xs, hs, vector_ref, residual_ref, energy_ref, out_buf, out_sem):
    block = xs.shape[-1]

    def copies(v, spin):
        return [
            pltpu.make_async_copy(
                out_buf.at[which, v, spin], target.at[0, v, 0, spin], out_sem.at[which, v, spin]
            )
            for which, target in enumerate((vector_ref, residual_ref))
        ]

    for v in range(2):
        cosine, from_second, energy = [scalar_ref[v, k : k + 1, 0:1] for k in range(3)]
        for spin in range(4):

            def step(i, carry, v=v, spin=spin):
                rows = pl.ds(pl.multiple_of(i * 32, 32), 32)
                ritz = cosine * xs[v, spin, rows, :].astype(F32)
                ritz = ritz + from_second * xs[v + 2, spin, rows, :].astype(F32)
                out_buf[0, v, spin, rows, :] = ritz
                out_buf[1, v, spin, rows, :] = (
                    cosine * hs[v, spin, rows, :]
                    + from_second * hs[v + 2, spin, rows, :]
                    - energy * ritz
                )
                return carry

            lax.fori_loop(0, block // 32, step, 0)
            for copy in copies(v, spin):
                copy.start()
        energy_ref[0, v] = energy[0, 0]
    for v in range(2):
        for spin in range(4):
            for copy in copies(v, spin):
                copy.wait()


def body(start_vectors, left_env, right_env, pair_mpo):
    block = start_vectors.shape[-1]
    count = lax.axis_size("sec")
    sizes = grid_sizes(count)
    wide = (1, 2, 1, 4, block, block)
    any_spec = pl.BlockSpec(memory_space=pl.ANY)
    vmem_spec = pl.BlockSpec(memory_space=pltpu.VMEM)
    dma = pltpu.SemaphoreType.DMA
    vectors, images, scalars = pl.pallas_call(
        lambda *refs: kernel(sizes, *refs),
        name="davidson",
        out_shape=(
            pltpu.VMEM((4, 4, block, block), BF16),
            pltpu.VMEM((4, 4, block, block), F32),
            pltpu.VMEM((2, 8, 128), F32),
        ),
        in_specs=[vmem_spec, any_spec, any_spec, any_spec],
        out_specs=(vmem_spec, vmem_spec, vmem_spec),
        scratch_shapes=[
            pltpu.VMEM((2, 4, block, block), BF16),
            pltpu.VMEM((2, 4, 5, block, block), F32),
            pltpu.VMEM((3, 5, block, block), BF16),
            pltpu.VMEM((block, 5 * block), BF16),
            pltpu.VMEM((4, 3 * block, block), BF16),
            pltpu.VMEM((4, 2, 4, block, block), BF16),
            pltpu.VMEM((4, 4, 2 * block, block), BF16),
            pltpu.VMEM((2, 3, 8, 128), F32),
            pltpu.SMEM((len(COEFS),), F32),
            dma((2,)),
            dma((3, 2)),
            dma((3, 2)),
            dma((5,)),
            dma((5,)),
            dma((4, 2, 8)),
            dma((4, 2, 8)),
            dma((4, len(sizes), max(sizes))),
            dma((4, len(sizes), max(sizes))),
            *[pltpu.VMEM((4, size, 1, 128), F32) for size in sizes],
        ],
        compiler_params=pltpu.CompilerParams(
            collective_id=0, has_side_effects=True, vmem_limit_bytes=48 * 1024 * 1024
        ),
    )(jnp.transpose(pair_mpo, (0, 2, 3, 1)), start_vectors, left_env, right_env)

    return pl.pallas_call(
        combine,
        name="combine",
        out_shape=(
            jax.ShapeDtypeStruct(wide, F32),
            jax.ShapeDtypeStruct(wide, F32),
            jax.ShapeDtypeStruct((1, 2), F32),
        ),
        in_specs=[vmem_spec, vmem_spec, vmem_spec],
        out_specs=(any_spec, any_spec, pl.BlockSpec(memory_space=pltpu.SMEM)),
        scratch_shapes=[pltpu.VMEM((2, 2, 4, block, block), F32), dma((2, 2, 4))],
        compiler_params=pltpu.CompilerParams(vmem_limit_bytes=16 * 1024 * 1024),
    )(scalars, vectors, images)


def solution(mesh):
    in_specs = (
        P("sect", None, "sec", None, None, None),
        P("sect", "sec", None, None, None),
        P("sect", "sec", None, None, None),
        P(),
    )
    out_specs = (
        P("sect", None, "sec", None, None, None),
        P("sect", None, "sec", None, None, None),
        P("sect", None),
    )
    return jax.shard_map(body, mesh=mesh, in_specs=in_specs, out_specs=out_specs, check_vma=False)
```

```python
import jax
import jax.numpy as jnp
from jax import lax
from jax.experimental import pallas as pl
from jax.experimental.pallas import tpu as pltpu
from jax.sharding import PartitionSpec as P

MESH = pl.DeviceIdType.MESH
F32 = jnp.float32
BF16 = jnp.bfloat16
EPSILON = 1e-06
CHARGE = (0, 1, 1, 2)
SHIFT = (0, 0, 0, 1, -1)
SLOT_OF = {0: 0, 3: 1, 1: 2, 2: 3}
SPIN_OF = (0, 3, 1, 2)


def couplings(spin, channel, spin_in):
    change = CHARGE[spin] - CHARGE[spin_in]
    return [w2 for w2 in range(5) if change == SHIFT[channel] - SHIFT[w2]]


COEFS = [
    (w2, spin, channel, spin_in)
    for spin in range(4)
    for channel in range(5)
    for spin_in in range(4)
    for w2 in couplings(spin, channel, spin_in)
]
COEF_AT = {key: index for index, key in enumerate(COEFS)}


def grid_sizes(count):
    return {128: (16, 8), 8: (4, 2)}[count]


def folded_rows(value):
    return jnp.sum(value, axis=0, keepdims=True)


def folded(value):
    rows, columns = value.shape
    value = value.reshape(rows // 8, 8, columns).sum(axis=0)
    total = value[:, :128]
    for start in range(128, columns, 128):
        total = total + value[:, start : start + 128]
    return total


def whole(value):
    return jnp.sum(jnp.sum(value, axis=1, keepdims=True), axis=0, keepdims=True)


def kernel(
    sizes,
    mpo_ref,
    start_ref,
    left_ref,
    right_ref,
    xs,
    hs,
    scalar_ref,
    us,
    part,
    right_buf,
    left_buf,
    blended,
    send_buf,
    recv_buf,
    kept,
    coef,
    in_sem,
    r_send,
    r_recv,
    l_send,
    l_recv,
    b_send,
    b_recv,
    ar_send,
    ar_recv,
    *sums,
):
    count = 1
    for size in sizes:
        count *= size
    block = start_ref.shape[-1]
    step_rows = 32
    sect = lax.axis_index("sect")
    sec = lax.axis_index("sec")
    other = 1 - sect
    up = lax.rem(sec + 1, count)
    down = lax.rem(sec + count - 1, count)
    stages = []
    stride = 1
    for size in sizes:
        stages.append((size, stride, lax.rem(sec // stride, size)))
        stride *= size

    partners = [
        [
            (lax.rem(digit + k, size), sec + (lax.rem(digit + k, size) - digit) * stride)
            for k in range(size)
        ]
        for size, stride, digit in stages
    ]

    def partner(stage, k):
        return partners[stage][k]

    def far_first(size):
        inner = 4 if size == 16 else size
        return sorted(
            range(1, size),
            key=lambda k: -min(k % inner, inner - k % inner) - min(k // inner, size // inner - k // inner),
        )

    def device(section, sector):
        return {"sect": section, "sec": sector}

    def remote(source, target, send_sem, recv_sem, where):
        return pltpu.make_async_remote_copy(
            src_ref=source,
            dst_ref=target,
            send_sem=send_sem,
            recv_sem=recv_sem,
            device_id=where,
            device_id_type=MESH,
        )

    barrier = pltpu.get_barrier_semaphore()
    greeted = [device(other, sec), device(other, up), device(other, down)]
    greeted += [device(sect, up), device(sect, down)]
    for stage, size in enumerate(sizes):
        greeted += [device(sect, partner(stage, k)[1]) for k in range(1, size)]
    for where in greeted:
        pl.semaphore_signal(barrier, inc=1, device_id=where, device_id_type=MESH)
    loads = [
        pltpu.make_async_copy(start_ref.at[0, v, 0], us.at[v], in_sem.at[v]) for v in range(2)
    ]
    for load in loads:
        load.start()


    def right_copy(slot, part):
        first, last = ((3, 5), (0, 3))[part]
        return remote(
            right_ref.at[0, 0, first:last],
            right_buf.at[slot, first:last],
            r_send.at[slot, part],
            r_recv.at[slot, part],
            device(other, (up, sec, down)[slot]),
        )

    def left_copy(channel):
        return remote(
            left_ref.at[0, 0, channel],
            left_buf.at[:, channel * block : (channel + 1) * block],
            l_send.at[channel],
            l_recv.at[channel],
            device(other, sec),
        )

    right_copies = [right_copy(*k) for k in ((0, 0), (2, 0), (1, 0), (1, 1), (0, 1), (2, 1))]
    left_copies = [left_copy(channel) for channel in range(5)]

    def multiply(phase, v, spins, channels):
        low, high = spins
        first, last = channels
        right = right_buf[CHARGE[low], first:last].reshape((last - first) * block, block)
        vectors = xs[phase, low:high].reshape((high - low) * block, block)
        product = lax.dot_general(
            vectors, right, (((1,), (1,)), ((), ())), preferred_element_type=F32
        )
        for spin_in in range(low, high):
            for w2 in range(first, last):
                part[v, spin_in, w2] = product[
                    (spin_in - low) * block : (spin_in - low + 1) * block,
                    (w2 - first) * block : (w2 - first + 1) * block,
                ]

    def multiply_all(phase, v):
        multiply(phase, v, (1, 3), (0, 5))
        multiply(phase, v, (0, 1), (0, 5))
        multiply(phase, v, (3, 4), (0, 5))

    def multiply_early(phase, v):
        multiply(phase, v, (0, 1), (3, 5))
        multiply(phase, v, (3, 4), (3, 5))
        multiply(phase, v, (1, 3), (0, 3))

    def multiply_late(phase, v):
        multiply(phase, v, (0, 1), (0, 3))
        multiply(phase, v, (3, 4), (0, 3))
        multiply(phase, v, (1, 3), (3, 5))

    def mix(v, targets, store):
        def step(i, carry):
            rows = pl.ds(pl.multiple_of(i * 16, 16), 16)
            held = {}
            for spin, channel in targets:
                total = None
                for spin_in in range(4):
                    for w2 in couplings(spin, channel, spin_in):
                        key = (spin_in, w2)
                        if key not in held:
                            held[key] = part[v, spin_in, w2, rows, :]
                        term = coef[COEF_AT[(w2, spin, channel, spin_in)]] * held[key]
                        total = term if total is None else total + term
                store(spin, channel, rows, i, total.astype(BF16))
            return carry

        lax.fori_loop(0, block // 16, step, 0)

    def block_copy(phase, side, piece):
        return remote(
            send_buf.at[phase, side, piece],
            recv_buf.at[phase, piece, side * block : (side + 1) * block],
            b_send.at[phase, side, piece],
            b_recv.at[phase, side, piece],
            device(sect, (down, up)[side]),
        )

    def produce(phase, v, half):
        def store(spin, channel, rows, i, value):
            send_buf[phase, channel - 3, SLOT_OF[spin], rows, :] = value

        mix(v, [(spin, w) for spin in ((0, 3), (1, 2))[half] for w in (3, 4)], store)

    def send(phase, first, last):
        for piece in range(first, last):
            for side in range(2):
                block_copy(phase, side, piece).start()

    def local(phase, v):
        def store(spin, channel, rows, i, value):
            start = pl.multiple_of(channel * block + i * 16, 16)
            blended[spin, pl.ds(start, 16), :] = value

        for channel in range(3):
            mix(v, [(spin, channel) for spin in range(4)], store)
        for spin in range(4):
            hs[phase, spin] = jnp.dot(
                left_buf[:, : 3 * block], blended[spin], preferred_element_type=F32
            )

    def spin_rows(spin, function, total):
        def step(i, carry):
            rows = pl.ds(pl.multiple_of(i * step_rows, step_rows), step_rows)
            return function(spin, rows, carry)

        return lax.fori_loop(0, block // step_rows, step, total)

    def over_rows(function, total):
        for spin in range(4):
            total = spin_rows(spin, function, total)
        return total

    def consume(phase, function, total):
        for slot in range(4):
            for side in range(2):
                block_copy(phase, side, slot).wait_recv()
            spin = SPIN_OF[slot]
            hs[phase, spin] += jnp.dot(
                left_buf[:, 3 * block :],
                recv_buf[phase, slot],
                preferred_element_type=F32,
            )
            total = spin_rows(spin, function, total)
        return total

    zero = jnp.zeros((8, 128), F32)

    def sum_copies(phase):
        def copy_to(stage, k):
            digit = stages[stage][2]
            return remote(
                sums[stage].at[phase, digit],
                sums[stage].at[phase, digit],
                ar_send.at[phase, stage, k],
                ar_recv.at[phase, stage, digit],
                device(sect, partner(stage, k)[1]),
            )

        def copy_from(stage, k):
            there, sector = partner(stage, k)
            return remote(
                sums[stage].at[phase, there],
                sums[stage].at[phase, there],
                ar_send.at[phase, stage, k],
                ar_recv.at[phase, stage, there],
                device(sect, sector),
            )

        return copy_to, copy_from

    def send_sums(phase, stage, total):
        copy_to, _ = sum_copies(phase)
        size, _, digit = stages[stage]
        sums[stage][phase, digit] = total
        for k in far_first(size):
            copy_to(stage, k).start()

    def take_sums(phase, stage):
        _, copy_from = sum_copies(phase)
        size = sizes[stage]
        for k in range(1, size):
            copy_from(stage, k).wait_recv()
        total = sums[stage][phase, 0]
        for index in range(1, size):
            total = total + sums[stage][phase, index]
        return total

    def begin_sum(phase, values):
        rows = [folded_rows(value) for value in values]
        rows.append(jnp.zeros((8 - len(rows), 128), F32))
        tile = jnp.sum(jnp.concatenate(rows, axis=0), axis=1, keepdims=True)
        lane = lax.broadcasted_iota(jnp.int32, (8, 128), 1)
        place = lax.broadcasted_iota(jnp.int32, (8, 128), 0)
        spread = jnp.where(lane == place, jnp.broadcast_to(tile, (8, 128)), 0.0)
        send_sums(phase, 0, jnp.sum(spread, axis=0, keepdims=True))

    def pass_sum(phase):
        for stage in range(1, len(sizes)):
            send_sums(phase, stage, take_sums(phase, stage - 1))

    def end_sum(phase):
        total = take_sums(phase, len(sizes) - 1)
        return [total[:, k : k + 1] for k in range(6)]

    def start_block(v, spin, rows):
        value = us[v, spin, rows, :].astype(F32)
        if spin == 0:
            value = value * jnp.where(sec == 0, 0.0, 1.0).astype(F32)
        if spin == 3:
            value = value * jnp.where(sec == count - 1, 0.0, 1.0).astype(F32)
        return value

    def start_sum(v):
        def step(spin, rows, carry):
            value = start_block(v, spin, rows)
            return carry + folded(value * value)

        return over_rows(step, zero)

    def make_first(v, start_sq):
        inv_norm = 1.0 / jnp.sqrt(start_sq + EPSILON)

        def step(spin, rows, carry):
            xs[v, spin, rows, :] = (start_block(v, spin, rows) * inv_norm).astype(BF16)
            return carry

        over_rows(step, 0)

    def first_sums(v):
        def step(spin, rows, carry):
            squared, product, image_sq = carry
            x = xs[v, spin, rows, :].astype(F32)
            image = hs[v, spin, rows, :]
            return (
                squared + folded(x * x),
                product + folded(x * image),
                image_sq + folded(image * image),
            )

        return consume(v, step, (zero, zero, zero))

    def make_second(v, squared, rayleigh, image_sq):
        estimate = image_sq - 2.0 * rayleigh * rayleigh + rayleigh * rayleigh * squared
        norm = jnp.sqrt(jnp.maximum(estimate, 0.0) + EPSILON)
        inv_norm = 1.0 / norm

        def step(spin, rows, carry):
            x = xs[v, spin, rows, :].astype(F32)
            value = hs[v, spin, rows, :] - rayleigh * x
            xs[v + 2, spin, rows, :] = (value * inv_norm).astype(BF16)
            return carry + folded(value * value)

        kept[v, 0] = jnp.broadcast_to(rayleigh, (8, 128))
        kept[v, 1] = jnp.broadcast_to(norm, (8, 128))
        kept[v, 2] = over_rows(step, zero)

    def second_sums(v):
        def step(spin, rows, carry):
            mixed, diagonal = carry
            x = xs[v, spin, rows, :].astype(F32)
            image = hs[v + 2, spin, rows, :]
            second = xs[v + 2, spin, rows, :].astype(F32)
            return mixed + folded(x * image), diagonal + folded(second * image)

        return consume(v + 2, step, (zero, zero))

    def finish(v, residual_sq, coupling_raw, diagonal_raw):
        rayleigh = kept[v, 0, 0:1, 0:1]
        scale = kept[v, 1, 0:1, 0:1] / jnp.sqrt(residual_sq + EPSILON)
        coupling = coupling_raw * scale
        second_diag = diagonal_raw * scale * scale
        half_gap = 0.5 * (second_diag - rayleigh)
        radius = jnp.sqrt(half_gap * half_gap + coupling * coupling)
        energy = 0.5 * (rayleigh + second_diag) - radius
        flat = radius <= 0.0
        safe = jnp.where(flat, 1.0, radius)
        larger = jnp.sqrt(0.5 * (1.0 + jnp.abs(half_gap) / safe))
        smaller = 0.5 * jnp.abs(coupling) / (safe * larger)
        ahead = half_gap >= 0.0
        sign = jnp.where(coupling < 0.0, -1.0, 1.0)
        cosine = jnp.where(flat, 1.0, jnp.where(ahead, larger, smaller))
        sine = jnp.where(flat, 0.0, sign * jnp.where(ahead, smaller, larger))
        from_second = -sine * scale

        for row, value in enumerate((cosine, from_second, energy)):
            scalar_ref[v, row : row + 1, :] = jnp.broadcast_to(value, (1, 128))

    for load in loads:
        load.wait()
    start_sq = [start_sum(v) for v in range(2)]
    pl.semaphore_wait(barrier, len(greeted))
    begin_sum(0, start_sq)
    for copy in right_copies[:4] + left_copies:
        copy.start()
    for (w2, spin, channel, spin_in), index in COEF_AT.items():
        there = sec + (CHARGE[spin_in] - 1)
        origin = there - SHIFT[w2]
        keep = (there >= 0) & (there < count) & (origin >= 0) & (origin < count)
        coef[index] = mpo_ref[channel, spin][spin_in, w2] * jnp.where(keep, 1.0, 0.0).astype(F32)

    pass_sum(0)
    for copy in right_copies[4:]:
        copy.start()
    right_copy(1, 0).wait_recv()
    right_copy(1, 1).wait_recv()
    start_sq = end_sum(0)
    make_first(0, start_sq[0])

    multiply(0, 0, (1, 3), (0, 5))
    right_copy(0, 0).wait_recv()
    right_copy(2, 0).wait_recv()
    multiply(0, 0, (0, 1), (3, 5))
    multiply(0, 0, (3, 4), (3, 5))
    produce(0, 0, 0)
    send(0, 0, 2)
    make_first(1, start_sq[1])
    right_copy(0, 1).wait_recv()
    right_copy(2, 1).wait_recv()
    multiply(0, 0, (0, 1), (0, 3))
    multiply(0, 0, (3, 4), (0, 3))
    produce(0, 0, 1)
    send(0, 2, 4)
    multiply_all(1, 1)
    produce(1, 1, 0)
    send(1, 0, 1)
    produce(1, 1, 1)
    for copy in left_copies:
        copy.wait_recv()

    @pl.when(sec == count - 1)
    def _():
        left_buf[:, 3 * block : 4 * block] = jnp.zeros((block, block), BF16)

    @pl.when(sec == 0)
    def _():
        left_buf[:, 4 * block :] = jnp.zeros((block, block), BF16)

    local(0, 0)
    begin_sum(1, first_sums(0))
    send(1, 1, 3)
    local(1, 1)
    pass_sum(1)
    send(1, 3, 4)
    first = end_sum(1)
    begin_sum(2, first_sums(1))
    make_second(0, *first[:3])

    multiply_early(2, 0)
    produce(2, 0, 0)
    send(2, 0, 2)
    multiply_late(2, 0)
    produce(2, 0, 1)
    pass_sum(2)
    send(2, 2, 4)
    local(2, 0)
    make_second(1, *end_sum(2)[:3])
    multiply_early(3, 1)
    produce(3, 1, 0)
    send(3, 0, 2)
    multiply_late(3, 1)
    produce(3, 1, 1)
    send(3, 2, 4)
    local(3, 1)
    first = (kept[0, 2], *second_sums(0))
    begin_sum(3, (*first, kept[1, 2], *second_sums(1)))

    def blocks_sent(phase, carry):
        for piece in range(4):
            for side in range(2):
                block_copy(phase, side, piece).wait_send()
        return carry

    lax.fori_loop(0, 4, blocks_sent, 0)
    for copy in right_copies + left_copies:
        copy.wait_send()

    def sums_sent(phase, carry):
        copy_to, _ = sum_copies(phase)
        for stage, size in enumerate(sizes):
            for k in range(1, size):
                copy_to(stage, k).wait_send()
        return carry

    lax.fori_loop(0, 3, sums_sent, 0)

    pass_sum(3)
    final = end_sum(3)
    finish(0, *final[:3])
    finish(1, *final[3:])
    sums_sent(3, 0)


def combine(scalar_ref, xs, hs, vector_ref, residual_ref, energy_ref, out_buf, out_sem):
    block = xs.shape[-1]

    def copies(v, spin):
        return [
            pltpu.make_async_copy(
                out_buf.at[which, v, spin], target.at[0, v, 0, spin], out_sem.at[which, v, spin]
            )
            for which, target in enumerate((vector_ref, residual_ref))
        ]

    for v in range(2):
        cosine, from_second, energy = [scalar_ref[v, k : k + 1, 0:1] for k in range(3)]
        for spin in range(4):

            def step(i, carry, v=v, spin=spin):
                rows = pl.ds(pl.multiple_of(i * 32, 32), 32)
                ritz = cosine * xs[v, spin, rows, :].astype(F32)
                ritz = ritz + from_second * xs[v + 2, spin, rows, :].astype(F32)
                out_buf[0, v, spin, rows, :] = ritz
                out_buf[1, v, spin, rows, :] = (
                    cosine * hs[v, spin, rows, :]
                    + from_second * hs[v + 2, spin, rows, :]
                    - energy * ritz
                )
                return carry

            lax.fori_loop(0, block // 32, step, 0)
            for copy in copies(v, spin):
                copy.start()
        energy_ref[0, v] = energy[0, 0]
    for v in range(2):
        for spin in range(4):
            for copy in copies(v, spin):
                copy.wait()


def body(start_vectors, left_env, right_env, pair_mpo):
    block = start_vectors.shape[-1]
    count = lax.axis_size("sec")
    sizes = grid_sizes(count)
    wide = (1, 2, 1, 4, block, block)
    any_spec = pl.BlockSpec(memory_space=pl.ANY)
    vmem_spec = pl.BlockSpec(memory_space=pltpu.VMEM)
    dma = pltpu.SemaphoreType.DMA
    vectors, images, scalars = pl.pallas_call(
        lambda *refs: kernel(sizes, *refs),
        name="davidson",
        out_shape=(
            pltpu.VMEM((4, 4, block, block), BF16),
            pltpu.VMEM((4, 4, block, block), F32),
            pltpu.VMEM((2, 8, 128), F32),
        ),
        in_specs=[vmem_spec, any_spec, any_spec, any_spec],
        out_specs=(vmem_spec, vmem_spec, vmem_spec),
        scratch_shapes=[
            pltpu.VMEM((2, 4, block, block), BF16),
            pltpu.VMEM((2, 4, 5, block, block), F32),
            pltpu.VMEM((3, 5, block, block), BF16),
            pltpu.VMEM((block, 5 * block), BF16),
            pltpu.VMEM((4, 3 * block, block), BF16),
            pltpu.VMEM((4, 2, 4, block, block), BF16),
            pltpu.VMEM((4, 4, 2 * block, block), BF16),
            pltpu.VMEM((2, 3, 8, 128), F32),
            pltpu.SMEM((len(COEFS),), F32),
            dma((2,)),
            dma((3, 2)),
            dma((3, 2)),
            dma((5,)),
            dma((5,)),
            dma((4, 2, 4)),
            dma((4, 2, 4)),
            dma((4, len(sizes), max(sizes))),
            dma((4, len(sizes), max(sizes))),
            *[pltpu.VMEM((4, size, 1, 128), F32) for size in sizes],
        ],
        compiler_params=pltpu.CompilerParams(
            collective_id=0, has_side_effects=True, vmem_limit_bytes=48 * 1024 * 1024
        ),
    )(jnp.transpose(pair_mpo, (0, 2, 3, 1)), start_vectors, left_env, right_env)

    return pl.pallas_call(
        combine,
        name="combine",
        out_shape=(
            jax.ShapeDtypeStruct(wide, F32),
            jax.ShapeDtypeStruct(wide, F32),
            jax.ShapeDtypeStruct((1, 2), F32),
        ),
        in_specs=[vmem_spec, vmem_spec, vmem_spec],
        out_specs=(any_spec, any_spec, pl.BlockSpec(memory_space=pltpu.SMEM)),
        scratch_shapes=[pltpu.VMEM((2, 2, 4, block, block), F32), dma((2, 2, 4))],
        compiler_params=pltpu.CompilerParams(vmem_limit_bytes=16 * 1024 * 1024),
    )(scalars, vectors, images)


def solution(mesh):
    in_specs = (
        P("sect", None, "sec", None, None, None),
        P("sect", "sec", None, None, None),
        P("sect", "sec", None, None, None),
        P(),
    )
    out_specs = (
        P("sect", None, "sec", None, None, None),
        P("sect", None, "sec", None, None, None),
        P("sect", None),
    )
    return jax.shard_map(body, mesh=mesh, in_specs=in_specs, out_specs=out_specs, check_vma=False)
```
